768 devices in a mesh: curve: 128 (over z_hi, y, x), dp: 6 (over z_lo, core).
Axes of the slice: x: 4, y: 8, z: 12 (z_hi: 4, z_lo: 3; z = z_hi * 3 + z_lo), core: 2. Of those that a mesh axis runs over, the one named last changes fastest.
Arguments:
- queries: bfloat16 [32768, 3072], P('curve', 'dp'), may hold values from -40 to 40
- keys: bfloat16 [32768, 3072], P('curve', 'dp'), may hold values from -40 to 40
- values: bfloat16 [32768, 3072], P('curve', 'dp'), may hold values from -64 to 64
- cotangent: bfloat16 [32768, 3072], P('curve', 'dp'), may hold values from -6 to 6
- gain: float32 [3072], P('dp'), may hold values from 0.5 to 1.5
- neighbour_ids: int32 [256, 3], replicated, may hold values from 0 to 255, as said below
- neighbour_counts: int32 [256], replicated, may hold values from 1 to 3, as said below
Outputs:
- normed: bfloat16 [32768, 3072], P('curve', 'dp')
- grad_queries: bfloat16 [32768, 3072], P('curve', 'dp')
- grad_keys: bfloat16 [32768, 3072], P('curve', 'dp')
- grad_values: bfloat16 [32768, 3072], P('curve', 'dp')
The draws below stay inside these ranges and needn't reach their ends.
Inputs may be any that keep to these rules, and one draw needn't show every extreme that they name: `neighbour_ids`: row a belongs to query block a: slot 0 holds a; slots 1 to neighbour_counts[a] - 1 hold distinct blocks b other than a with |b - a| <= 1; later slots hold a. `neighbour_counts`: the number of used slots of each row of neighbour_ids.
All inputs are finite; a program needn't handle non-finite values.
Results may differ from the reference program's by a relative error of at most 0.017.
Values may be sent and summed in bfloat16 or wider, within the bound.
No kernel may reach another device: no remote copies, remote signals or barrier semaphores. Data moves between devices by JAX's collectives and lax.ppermute only.
A program may use at most 32 MiB of HBM per device.

```python
import math
import jax
import jax.numpy as jnp
from jax import lax

HEADS = 24
HD = 128
BLK = 128
RIM = 1
GB = 2
QB = 2
NBR = 3
BLOCKS = 256
TOKENS = 32768
FEAT = 3072


def draw_queries(key, part):
    result = jax.random.normal(jax.random.fold_in(key, 1), (TOKENS, FEAT), jnp.float32)
    result = jnp.clip(result, -6.0, 6.0)
    return jnp.clip(result, -40.0, 40.0).astype(jnp.bfloat16)


def draw_keys(key, part):
    result = jax.random.normal(jax.random.fold_in(key, 2), (TOKENS, FEAT), jnp.float32)
    result = jnp.clip(result, -6.0, 6.0)
    return jnp.clip(result, -40.0, 40.0).astype(jnp.bfloat16)


def draw_values(key, part):
    heads = (jnp.arange(FEAT) // HD).astype(jnp.float32)
    ramp = heads / (HEADS - 1)
    drawn = jax.random.normal(jax.random.fold_in(key, 3), (TOKENS, FEAT), jnp.float32)
    result = jnp.clip(drawn, -6.0, 6.0) * jnp.power(10.0, ramp)[None, :]
    return jnp.clip(result, -64.0, 64.0).astype(jnp.bfloat16)


def neighbour_lists(key):
    blocks = jnp.arange(BLOCKS, dtype=jnp.int32)
    shard = blocks // QB
    level = jax.random.randint(jax.random.fold_in(key, 21), (BLOCKS // QB,), 1, NBR + 1)[shard]
    target = jax.random.randint(jax.random.fold_in(key, 22), (BLOCKS,), 1, NBR + 1)
    target = jnp.minimum(target, level)
    middle = QB * (BLOCKS // QB // 2) + QB // 2
    target = jnp.where(blocks == middle, NBR, target)
    last_edge = BLOCKS - QB - 1
    first_edge = QB
    target = jnp.where((blocks == last_edge) | (blocks == first_edge), NBR, target)
    offsets = jnp.concatenate([jnp.arange(-RIM, 0, dtype=jnp.int32), jnp.arange(1, RIM + 1, dtype=jnp.int32)])
    width = 2 * RIM
    candidates = blocks[:, None] + offsets[None, :]
    inside = (candidates >= 0) & (candidates < BLOCKS)
    rank = jnp.arange(width, dtype=jnp.int32)
    priority = jax.random.randint(jax.random.fold_in(key, 23), (BLOCKS, width), 0, 1 << 20) * width + rank[None, :]
    priority = jnp.where(inside, priority, (1 << 26) + rank[None, :])
    order = jnp.argsort(priority, axis=1, stable=True)
    picked = jnp.take_along_axis(candidates, order, axis=1)
    available = jnp.sum(inside.astype(jnp.int32), axis=1)
    extra = jnp.minimum(target - 1, available)
    slot = jnp.arange(1, NBR, dtype=jnp.int32)
    rest = jnp.where(slot[None, :] <= extra[:, None], picked, blocks[:, None])
    ids = jnp.concatenate([blocks[:, None], rest], axis=1)
    return (ids.astype(jnp.int32), (1 + extra).astype(jnp.int32))


def draw_neighbour_ids(key, part):
    return neighbour_lists(key)[0]


def draw_neighbour_counts(key, part):
    return neighbour_lists(key)[1]


def levels(own_key, shape, cuts, smallest, top_value):
    loudness = 1.0
    for position, blocks in cuts:
        draws = jax.random.uniform(jax.random.fold_in(jax.random.fold_in(own_key, 6), position), (blocks,), jnp.float32, smallest / len(cuts), top_value / len(cuts))
        loudness = loudness * jnp.repeat(jnp.exp(draws), shape[position] // blocks).reshape((-1,) + (1,) * (len(shape) - 1 - position))
    return loudness


def gaussian(rng, shape, scale, bound, split=(), kind=jnp.bfloat16):
    values = jax.random.normal(rng, shape, jnp.float32) * scale
    if len(split) > 0:
        values = levels(rng, shape, split, -0.22, 0.18) * values
    return jnp.clip(values, min=-bound, max=bound).astype(kind)


def setup_inputs(seed: int = 0) -> dict:
    splits = jax.random.split(jax.random.key(seed), 8)
    return {
        "queries": draw_queries(jax.random.fold_in(splits[7], 71), 0),
        "keys": draw_keys(jax.random.fold_in(splits[7], 71), 0),
        "values": draw_values(jax.random.fold_in(splits[7], 71), 0),
        "cotangent": gaussian(splits[3], (TOKENS, FEAT), 1.0, 6.0, ((0, 128), (1, 6))),
        "gain": jnp.clip(1.0 + 0.1 * jax.random.normal(splits[4], (FEAT,), jnp.float32), 0.5, 1.5),
        "neighbour_ids": draw_neighbour_ids(jax.random.fold_in(splits[7], 71), 0),
        "neighbour_counts": draw_neighbour_counts(jax.random.fold_in(splits[7], 71), 0),
    }


EPS = 1e-06

def pick_blocks(blocks, where_idx):
    chosen = blocks[where_idx]
    return chosen.reshape(where_idx.shape[0], where_idx.shape[1] * blocks.shape[1], blocks.shape[2], blocks.shape[3])

def rounded(array):
    return lax.optimization_barrier(array.astype(jnp.bfloat16)).astype(jnp.float32)

def reference(queries, keys, values, cotangent, gain, neighbour_ids, neighbour_counts):
    f32 = jnp.float32
    scale = 1.0 / math.sqrt(HD)
    q_blocks = queries.reshape(BLOCKS, BLK, HEADS, HD)
    k_blocks = keys.reshape(BLOCKS, BLK, HEADS, HD)
    v_blocks = values.reshape(BLOCKS, BLK, HEADS, HD)
    slots = jnp.arange(NBR, dtype=jnp.int32)
    usable_all = slots[None, :] < neighbour_counts[:, None]
    gain_f = gain.astype(f32)
    n_groups = BLOCKS // GB
    group_ids = jnp.arange(n_groups, dtype=jnp.int32)

    def group_inputs(start):
        ids = lax.dynamic_slice_in_dim(neighbour_ids, start, GB, 0)
        use = lax.dynamic_slice_in_dim(usable_all, start, GB, 0)
        key_group = pick_blocks(k_blocks, ids).astype(f32)
        value_group = pick_blocks(v_blocks, ids).astype(f32)
        query_group = lax.dynamic_slice_in_dim(q_blocks, start, GB, 0).astype(f32)
        scores = jnp.einsum('gqhe,gkhe->ghqk', query_group, key_group) * scale
        keep = jnp.repeat(use, BLK, axis=1)
        scores = jnp.where(keep[:, None, None, :], scores, -jnp.inf)
        return (query_group, key_group, value_group, scores)

    def forward_group(group):
        start = group * GB
        query_group, key_group, value_group, scores = group_inputs(start)
        top = lax.optimization_barrier(jnp.max(scores, axis=3, keepdims=True))
        log_total = top + jnp.log(lax.optimization_barrier(jnp.sum(jnp.exp(scores - top), axis=3, keepdims=True)))
        weights = rounded(jnp.exp(scores - log_total))
        attended = jnp.einsum('ghqk,gkhe->gqhe', weights, value_group).reshape(GB * BLK, FEAT)
        rinv = lax.rsqrt(lax.optimization_barrier(jnp.sum(attended * attended, axis=1, keepdims=True)) / FEAT + EPS)
        normed = (gain_f * attended * rinv).astype(jnp.bfloat16)
        upstream = lax.dynamic_slice_in_dim(cotangent, start * BLK, GB * BLK, 0).astype(f32)
        weighted = upstream * gain_f
        cross = lax.optimization_barrier(jnp.sum(weighted * attended, axis=1, keepdims=True)) / FEAT
        d_att = (weighted * rinv - attended * (rinv * rinv * rinv) * cross).astype(jnp.bfloat16)
        d_back = lax.optimization_barrier(d_att).astype(f32)
        delta = lax.optimization_barrier(jnp.sum((d_back * attended).reshape(GB * BLK, HEADS, HD), axis=2))
        lse_rows = log_total[..., 0].transpose(0, 2, 1).reshape(GB * BLK, HEADS)
        return (normed, d_att, lse_rows, delta)
    normed, d_all, lse_all, delta_all = lax.map(forward_group, group_ids)
    normed = normed.reshape(TOKENS, FEAT)
    d_all = d_all.reshape(TOKENS, FEAT)
    lse_all = lse_all.reshape(TOKENS, HEADS)
    delta_all = delta_all.reshape(TOKENS, HEADS)

    def query_grads(group):
        start = group * GB
        query_group, key_group, value_group, scores = group_inputs(start)
        lse = lax.dynamic_slice_in_dim(lse_all, start * BLK, GB * BLK, 0).reshape(GB, BLK, HEADS).transpose(0, 2, 1)
        delta = lax.dynamic_slice_in_dim(delta_all, start * BLK, GB * BLK, 0).reshape(GB, BLK, HEADS).transpose(0, 2, 1)
        dout = lax.dynamic_slice_in_dim(d_all, start * BLK, GB * BLK, 0).astype(f32).reshape(GB, BLK, HEADS, HD)
        probs = jnp.exp(scores - lse[..., None])
        dprob = jnp.einsum('gqhe,gkhe->ghqk', dout, value_group)
        dscore = rounded(probs * (dprob - delta[..., None]) * scale)
        grads = jnp.einsum('ghqk,gkhe->gqhe', dscore, key_group)
        return grads.reshape(GB * BLK, FEAT).astype(jnp.bfloat16)
    grad_queries = lax.map(query_grads, group_ids).reshape(TOKENS, FEAT)
    pad_rows = RIM * BLK
    q_pad = jnp.pad(queries, ((pad_rows, pad_rows), (0, 0)))
    d_pad = jnp.pad(d_all, ((pad_rows, pad_rows), (0, 0)))
    lse_pad = jnp.pad(lse_all, ((pad_rows, pad_rows), (0, 0)))
    delta_pad = jnp.pad(delta_all, ((pad_rows, pad_rows), (0, 0)))
    ids_pad = jnp.pad(neighbour_ids, ((RIM, RIM), (0, 0)), constant_values=-1)
    use_pad = jnp.pad(usable_all, ((RIM, RIM), (0, 0)))
    span = GB + 2 * RIM

    def key_grads(group):
        start = group * GB
        query_rows = lax.dynamic_slice_in_dim(q_pad, start * BLK, span * BLK, 0).astype(f32).reshape(span * BLK, HEADS, HD)
        dout_rows = lax.dynamic_slice_in_dim(d_pad, start * BLK, span * BLK, 0).astype(f32).reshape(span * BLK, HEADS, HD)
        lse = lax.dynamic_slice_in_dim(lse_pad, start * BLK, span * BLK, 0).T[:, :, None]
        delta = lax.dynamic_slice_in_dim(delta_pad, start * BLK, span * BLK, 0).T[:, :, None]
        ids = lax.dynamic_slice_in_dim(ids_pad, start, span, 0)
        use = lax.dynamic_slice_in_dim(use_pad, start, span, 0)
        targets = start + jnp.arange(GB, dtype=jnp.int32)
        hit = jnp.any(use[:, :, None] & (ids[:, :, None] == targets[None, None, :]), axis=1)
        keep = jnp.repeat(jnp.repeat(hit, BLK, axis=0), BLK, axis=1)
        key_rows = lax.dynamic_slice_in_dim(keys, start * BLK, GB * BLK, 0).astype(f32).reshape(GB * BLK, HEADS, HD)
        value_rows = lax.dynamic_slice_in_dim(values, start * BLK, GB * BLK, 0).astype(f32).reshape(GB * BLK, HEADS, HD)
        scores = jnp.einsum('qhe,khe->hqk', query_rows, key_rows) * scale
        scores = jnp.where(keep[None], scores, -jnp.inf)
        probs = jnp.exp(scores - lse)
        dprob = jnp.einsum('qhe,khe->hqk', dout_rows, value_rows)
        dscore = rounded(probs * (dprob - delta) * scale)
        weights = rounded(probs)
        grad_k = jnp.einsum('hqk,qhe->khe', dscore, query_rows).reshape(GB * BLK, FEAT).astype(jnp.bfloat16)
        grad_v = jnp.einsum('hqk,qhe->khe', weights, dout_rows).reshape(GB * BLK, FEAT).astype(jnp.bfloat16)
        return (grad_k, grad_v)
    grad_keys, grad_values = lax.map(key_grads, group_ids)
    return (normed, grad_queries, grad_keys.reshape(TOKENS, FEAT), grad_values.reshape(TOKENS, FEAT))
```

```python
import functools
import math

import jax
import jax.numpy as jnp
from jax import lax
from jax.experimental import pallas as pl
from jax.experimental.pallas import tpu as pltpu
from jax.sharding import PartitionSpec as P

FEAT = 3072
HD = 128
BLK = 128
NBR = 3
BLOCKS = 256
EPS = 1e-06
SCALE = 1.0 / math.sqrt(HD)
NEG = -1e30
F32 = jnp.float32
BF16 = jnp.bfloat16


def mm(a, b):
    return lax.dot_general(a, b, (((1,), (0,)), ((), ())), preferred_element_type=F32)


def mm_t(a, b):
    return lax.dot_general(a, b, (((1,), (1,)), ((), ())), preferred_element_type=F32)


def t_mm(a, b):
    return lax.dot_general(a, b, (((0,), (0,)), ((), ())), preferred_element_type=F32)


def sees(ids_ref, cnt_ref, a, b):
    inside = jnp.logical_and(a >= 0, a < BLOCKS)
    row = jnp.clip(a, 0, BLOCKS - 1)
    hit = jnp.bool_(False)
    for j in range(NBR):
        hit = jnp.logical_or(hit, jnp.logical_and(j < cnt_ref[row], ids_ref[row, j] == b))
    return jnp.where(jnp.logical_and(hit, inside), F32(0.0), F32(NEG))


def own_bias(ids_ref, cnt_ref, first):
    up = sees(ids_ref, cnt_ref, first, first + 1)
    down = sees(ids_ref, cnt_ref, first + 1, first)
    row = lax.broadcasted_iota(jnp.int32, (2 * BLK, 2 * BLK), 0) >= BLK
    col = lax.broadcasted_iota(jnp.int32, (2 * BLK, 2 * BLK), 1) >= BLK
    off = jnp.where(row, down, up)
    return jnp.where(row == col, F32(0.0), off)


def side_of(index, side):
    even = 1 - lax.rem(index, 2)
    edge = even if side == 0 else 1 - even
    return edge, 2 * edge - 1


def head_cols(h, base=0):
    return slice(base + h * HD, base + (h + 1) * HD)


def own_kernel(heads, ids_ref, cnt_ref, q_ref, k_ref, v_ref, c_ref, send0_ref, send1_ref, o_ref, lse_ref):
    index = lax.axis_index("curve")
    feat = heads * HD
    bias = own_bias(ids_ref, cnt_ref, 2 * index)
    lane = lax.broadcasted_iota(jnp.int32, (2 * BLK, 128), 1)
    stats = jnp.zeros((2 * BLK, 128), F32)
    for h in range(heads):
        hs = head_cols(h)
        s = mm_t(q_ref[:, hs], k_ref[:, hs]) * SCALE + bias
        top = jnp.max(s, axis=1, keepdims=True)
        p = jnp.exp(s - top)
        total = jnp.sum(p, axis=1, keepdims=True)
        o_ref[:, hs] = mm(p.astype(BF16), v_ref[:, hs]) / total
        stats = jnp.where(lax.rem(lane, heads) == h, top + jnp.log(total), stats)
    lse_ref[...] = stats
    hi = stats.astype(BF16).astype(F32)
    mid = (stats - hi).astype(BF16).astype(F32)
    low = stats - hi - mid
    parts = jnp.where(lane < heads, hi, jnp.where(lane < 2 * heads, mid, low))
    parts = jnp.where(lane < 3 * heads, parts, 0.0)
    stat_rows = parts.astype(BF16)
    lse_rows = (stat_rows[:BLK], stat_rows[BLK:])
    for side, send in enumerate((send0_ref, send1_ref)):
        edge, _ = side_of(index, side)
        rows = pl.ds(pl.multiple_of(edge * BLK, BLK), BLK)
        for n, ref in enumerate((k_ref, v_ref, q_ref, c_ref)):
            send[:, n * feat : (n + 1) * feat] = ref[rows, :]
        send[:, 4 * feat : 5 * feat] = o_ref[rows, :].astype(BF16)
        send[:, 5 * feat :] = jnp.where(edge == 1, lse_rows[1].astype(F32), lse_rows[0].astype(F32)).astype(BF16)


def merge(s, lse_part, o_part, values):
    top = jnp.maximum(jnp.max(s, axis=1, keepdims=True), lse_part)
    p = jnp.exp(s - top)
    rest = jnp.exp(lse_part - top)
    total = jnp.sum(p, axis=1, keepdims=True) + rest
    out = (mm(p.astype(BF16), values) + rest * o_part) / total
    return out, top + jnp.log(total)


def side_bias(ids_ref, cnt_ref, index, edge, step):
    block = 2 * index + edge
    return sees(ids_ref, cnt_ref, block, block + step), sees(ids_ref, cnt_ref, block + step, block)


def join_kernel(
    heads, ids_ref, cnt_ref, q_ref, k_ref, v_ref, c_ref, gain_ref, o_ref, lse_in_ref, recv0_ref, recv1_ref,
    a_ref, lse_ref, sums_ref,
):
    index = lax.axis_index("curve")
    feat = heads * HD
    lane = lax.broadcasted_iota(jnp.int32, (BLK, 128), 1)
    gain = gain_ref[...]
    for side, recv in enumerate((recv0_ref, recv1_ref)):
        edge, step = side_of(index, side)
        rows = pl.ds(pl.multiple_of(edge * BLK, BLK), BLK)
        out_bias, in_bias = side_bias(ids_ref, cnt_ref, index, edge, step)
        lse_own = lse_in_ref[rows, :]
        far = recv[:, 5 * feat :].astype(F32)
        far_rows = slice((2 + side) * BLK, (3 + side) * BLK)
        own_stats = jnp.zeros((BLK, 128), F32)
        far_stats = jnp.zeros((BLK, 128), F32)
        sq_own = jnp.zeros((BLK, HD), F32)
        cr_own = jnp.zeros((BLK, HD), F32)
        sq_far = jnp.zeros((BLK, HD), F32)
        cr_far = jnp.zeros((BLK, HD), F32)
        for h in range(heads):
            hs = head_cols(h)
            g = gain[:, hs]
            s = mm_t(q_ref[rows, hs], recv[:, head_cols(h)]) * SCALE + out_bias
            a, lse = merge(s, lse_own[:, h : h + 1], o_ref[rows, hs], recv[:, head_cols(h, feat)])
            a_ref[rows, hs] = a
            own_stats = jnp.where(lane == h, lse, own_stats)
            sq_own += a * a
            cr_own += c_ref[rows, hs].astype(F32) * g * a
            s = mm_t(recv[:, head_cols(h, 2 * feat)], k_ref[rows, hs]) * SCALE + in_bias
            far_lse = far[:, h : h + 1] + far[:, heads + h : heads + h + 1] + far[:, 2 * heads + h : 2 * heads + h + 1]
            a, lse = merge(s, far_lse, recv[:, head_cols(h, 4 * feat)].astype(F32), v_ref[rows, hs])
            a_ref[far_rows, hs] = a
            far_stats = jnp.where(lane == h, lse, far_stats)
            sq_far += a * a
            cr_far += recv[:, head_cols(h, 3 * feat)].astype(F32) * g * a
        lse_ref[rows, :] = own_stats
        lse_ref[far_rows, :] = far_stats
        for row, squares, crosses in ((edge, sq_own, cr_own), (2 + side, sq_far, cr_far)):
            both = jnp.where(
                lane == 0,
                jnp.sum(squares, axis=1, keepdims=True),
                jnp.sum(crosses, axis=1, keepdims=True),
            ).T
            for j in range(sums_ref.shape[0]):
                sums_ref[j, pl.ds(row, 1), :] = both[0:1]
                sums_ref[j, pl.ds(4 + row, 1), :] = both[1:2]


def grad_kernel(
    heads, ids_ref, cnt_ref, q_ref, k_ref, v_ref, c_ref, gain_ref, a_ref, lse_ref, recv0_ref, recv1_ref, sums_ref,
    normed_ref, gq_out, gk_out, gv_out, gq_ref, gk_ref, gv_ref, d_ref,
):
    index = lax.axis_index("curve")
    feat = heads * HD
    gain = gain_ref[...]
    total = jnp.sum(sums_ref[...], axis=0) / FEAT
    rinv = lax.rsqrt(total[0:4] + EPS)
    turn = rinv * rinv * rinv * total[4:8]
    columns = jnp.concatenate([rinv, turn, jnp.zeros((BLK - 8, 128), F32)], axis=0).T
    deltas = []
    for b in range(4):
        rows = slice(b * BLK, (b + 1) * BLK)
        a = a_ref[rows, :]
        r, t = columns[:, b : b + 1], columns[:, 4 + b : 5 + b]
        if b < 2:
            normed_ref[rows, :] = (gain * a * r).astype(BF16)
            cot = c_ref[rows, :]
        else:
            cot = (recv0_ref, recv1_ref)[b - 2][:, 3 * feat : 4 * feat]
        d = (cot.astype(F32) * gain * r - a * t).astype(BF16)
        d_ref[rows, :] = d
        both = d.astype(F32) * a
        deltas.append([jnp.sum(both[:, head_cols(h)], axis=1, keepdims=True) for h in range(heads)])
    bias = own_bias(ids_ref, cnt_ref, 2 * index)
    own = slice(0, 2 * BLK)
    for h in range(heads):
        hs = head_cols(h)
        q, k, v, d = q_ref[:, hs], k_ref[:, hs], v_ref[:, hs], d_ref[own, hs]
        delta = jnp.concatenate([deltas[0][h], deltas[1][h]], axis=0)
        p = jnp.exp(mm_t(q, k) * SCALE + bias - lse_ref[own, h : h + 1])
        ds = (p * (mm_t(d, v) - delta) * SCALE).astype(BF16)
        gq_ref[:, hs] = mm(ds, k)
        gk_ref[:, hs] = t_mm(ds, q)
        gv_ref[:, hs] = t_mm(p.astype(BF16), d)
    for side, recv in enumerate((recv0_ref, recv1_ref)):
        edge, step = side_of(index, side)
        rows = pl.ds(pl.multiple_of(edge * BLK, BLK), BLK)
        far_rows = slice((2 + side) * BLK, (3 + side) * BLK)
        out_bias, in_bias = side_bias(ids_ref, cnt_ref, index, edge, step)
        for h in range(heads):
            hs = head_cols(h)
            far_k, far_v, far_q = (recv[:, head_cols(h, n * feat)] for n in range(3))
            d = d_ref[rows, hs]
            delta = jnp.where(edge == 1, deltas[1][h], deltas[0][h])
            p = jnp.exp(mm_t(q_ref[rows, hs], far_k) * SCALE + out_bias - lse_ref[rows, h : h + 1])
            ds = (p * (mm_t(d, far_v) - delta) * SCALE).astype(BF16)
            gq_out[rows, hs] = (gq_ref[rows, hs] + mm(ds, far_k)).astype(BF16)
            d = d_ref[far_rows, hs]
            p = jnp.exp(mm_t(far_q, k_ref[rows, hs]) * SCALE + in_bias - lse_ref[far_rows, h : h + 1])
            ds = (p * (mm_t(d, v_ref[rows, hs]) - deltas[2 + side][h]) * SCALE).astype(BF16)
            gk_out[rows, hs] = (gk_ref[rows, hs] + t_mm(ds, far_q)).astype(BF16)
            gv_out[rows, hs] = (gv_ref[rows, hs] + t_mm(p.astype(BF16), d)).astype(BF16)


SMEM = pl.BlockSpec(memory_space=pltpu.SMEM)
VMEM = pl.BlockSpec(memory_space=pltpu.VMEM)
PARAMS = pltpu.CompilerParams(vmem_limit_bytes=32 * 1024 * 1024)


def call(kernel, name, n_vmem, outs, scratch=()):
    return pl.pallas_call(
        kernel,
        name=name,
        out_shape=outs,
        in_specs=[SMEM, SMEM] + [VMEM] * n_vmem,
        out_specs=tuple(VMEM for _ in outs),
        scratch_shapes=list(scratch),
        compiler_params=PARAMS,
    )


def shards(queries, keys, values, cotangent, gain, neighbour_ids, neighbour_counts):
    rows, feat = queries.shape
    heads = feat // HD
    count = lax.axis_size("curve")
    peers = lax.axis_size("dp")
    width = 5 * feat + 128
    shape = jax.ShapeDtypeStruct
    lists = (neighbour_ids, neighbour_counts)
    gain = gain.reshape(1, feat)
    send0, send1, o_own, lse_own = call(
        functools.partial(own_kernel, heads), "own", 4,
        (shape((BLK, width), BF16), shape((BLK, width), BF16), shape((rows, feat), F32), shape((rows, 128), F32)),
    )(*lists, queries, keys, values, cotangent)
    odd = [(i, i + 1) for i in range(1, count - 1, 2)]
    even = [(i, i + 1) for i in range(0, count, 2)]
    recv1 = lax.ppermute(send1, "curve", odd + [(b, a) for a, b in odd])
    recv0 = lax.ppermute(send0, "curve", even + [(b, a) for a, b in even])
    attended, lse, sums = call(
        functools.partial(join_kernel, heads), "join", 9,
        (shape((2 * rows, feat), F32), shape((2 * rows, 128), F32), shape((peers, 8, 128), F32)),
    )(*lists, queries, keys, values, cotangent, gain, o_own, lse_own, recv0, recv1)
    sums = lax.all_to_all(sums, "dp", 0, 0, tiled=True)
    return call(
        functools.partial(grad_kernel, heads), "grads", 10,
        tuple(shape((rows, feat), BF16) for _ in range(4)),
        [pltpu.VMEM((rows, feat), F32)] * 3 + [pltpu.VMEM((2 * rows, feat), BF16)],
    )(*lists, queries, keys, values, cotangent, gain, attended, lse, recv0, recv1, sums)


def solution(mesh):
    wide = P("curve", "dp")
    return jax.shard_map(
        shards,
        mesh=mesh,
        in_specs=(wide, wide, wide, wide, P("dp"), P(), P()),
        out_specs=(wide, wide, wide, wide),
        check_vma=False,
    )
```

```python
import functools
import math

import jax
import jax.numpy as jnp
from jax import lax
from jax.experimental import pallas as pl
from jax.experimental.pallas import tpu as pltpu
from jax.sharding import PartitionSpec as P

FEAT = 3072
HD = 128
BLK = 128
NBR = 3
BLOCKS = 256
EPS = 1e-06
SCALE = 1.0 / math.sqrt(HD)
NEG = -1e30
F32 = jnp.float32
BF16 = jnp.bfloat16


def mm(a, b):
    return lax.dot_general(a, b, (((1,), (0,)), ((), ())), preferred_element_type=F32)


def mm_t(a, b):
    return lax.dot_general(a, b, (((1,), (1,)), ((), ())), preferred_element_type=F32)


def t_mm(a, b):
    return lax.dot_general(a, b, (((0,), (0,)), ((), ())), preferred_element_type=F32)


def sees(ids_ref, cnt_ref, a, b):
    inside = jnp.logical_and(a >= 0, a < BLOCKS)
    row = jnp.clip(a, 0, BLOCKS - 1)
    hit = jnp.bool_(False)
    for j in range(NBR):
        hit = jnp.logical_or(hit, jnp.logical_and(j < cnt_ref[row], ids_ref[j, row] == b))
    return jnp.where(jnp.logical_and(hit, inside), F32(0.0), F32(NEG))


def own_bias(mask_ref):
    row = lax.broadcasted_iota(jnp.int32, (2 * BLK, 2 * BLK), 0) >= BLK
    col = lax.broadcasted_iota(jnp.int32, (2 * BLK, 2 * BLK), 1) >= BLK
    off = jnp.where(row, mask_ref[1], mask_ref[0])
    return jnp.where(row == col, F32(0.0), off)


def side_of(index, side):
    even = 1 - lax.rem(index, 2)
    edge = even if side == 0 else 1 - even
    return edge, 2 * edge - 1


def edge_rows(edge):
    return pl.ds(pl.multiple_of(edge * BLK, BLK), BLK)


def head_cols(h, base=0):
    return slice(base + h * HD, base + (h + 1) * HD)


def own_kernel(
    heads, ids_hbm, cnt_hbm, q_hbm, k_hbm, v_hbm, c_hbm, gain_hbm,
    send0_ref, send1_ref, chunk0_ref, chunk1_ref, o_ref, lse_ref, q_ref, k_ref, v_ref, c_ref, gain_ref, mask_ref,
    ids_ref, cnt_ref, sems,
):
    index = lax.axis_index("curve")
    feat = heads * HD
    copies = [
        pltpu.make_async_copy(src, dst, sems.at[n])
        for n, (src, dst) in enumerate(
            (
                (ids_hbm, ids_ref), (cnt_hbm, cnt_ref), (q_hbm, q_ref), (k_hbm, k_ref), (v_hbm, v_ref),
                (c_hbm, c_ref), (gain_hbm, gain_ref),
            )
        )
    ]
    for copy in copies:
        copy.start()
    for copy in copies[:2]:
        copy.wait()
    first = 2 * index
    mask_ref[0] = sees(ids_ref, cnt_ref, first, first + 1)
    mask_ref[1] = sees(ids_ref, cnt_ref, first + 1, first)
    for side in range(2):
        edge, step = side_of(index, side)
        block = first + edge
        mask_ref[2 + 2 * side] = sees(ids_ref, cnt_ref, block, block + step)
        mask_ref[3 + 2 * side] = sees(ids_ref, cnt_ref, block + step, block)
    bias = own_bias(mask_ref)
    for copy in copies[2:]:
        copy.wait()
    lane = lax.broadcasted_iota(jnp.int32, (2 * BLK, 128), 1)
    stats = jnp.zeros((2 * BLK, 128), F32)
    for h in range(heads):
        hs = head_cols(h)
        s = mm_t(q_ref[:, hs], k_ref[:, hs]) * SCALE + bias
        top = jnp.max(s, axis=1, keepdims=True)
        p = jnp.exp(s - top)
        total = jnp.sum(p, axis=1, keepdims=True)
        o_ref[:, hs] = mm(p.astype(BF16), v_ref[:, hs]) / total
        stats = jnp.where(lax.rem(lane, heads) == h, top + jnp.log(total), stats)
    lse_ref[...] = stats
    for side, send in enumerate((send0_ref, send1_ref)):
        edge, _ = side_of(index, side)
        rows = edge_rows(edge)
        for n, ref in enumerate((k_ref, v_ref, q_ref, c_ref)):
            send[:, n * feat : (n + 1) * feat] = ref[rows, :]
        send[:, 4 * feat : 5 * feat] = o_ref[rows, :].astype(BF16)
        lse = lse_ref[rows, :]
        lane = lax.broadcasted_iota(jnp.int32, (BLK, 128), 1)
        hi = lse.astype(BF16).astype(F32)
        mid = (lse - hi).astype(BF16).astype(F32)
        parts = jnp.where(lane < heads, hi, jnp.where(lane < 2 * heads, mid, lse - hi - mid))
        send[:, 5 * feat :] = parts.astype(BF16)
    cut = chunk0_ref.shape[1]
    chunk0_ref[...] = send1_ref[:, :cut]
    chunk1_ref[...] = send1_ref[:, cut:]


def stack(parts):
    return jnp.concatenate(parts, axis=0)


def join_kernel(
    heads, mask_ref, q_ref, k_ref, v_ref, c_ref, gain_ref, o_ref, lse_in_ref, recv0_ref, recv1_ref, chunk0_ref,
    chunk1_ref, a_ref, lse_ref, sums_ref, far_ref,
):
    index = lax.axis_index("curve")
    feat = heads * HD
    cut = chunk0_ref.shape[1]
    lane = lax.broadcasted_iota(jnp.int32, (BLK, 128), 1)
    far_ref[:, :cut] = recv1_ref[:, :cut] + chunk0_ref[...]
    far_ref[:, cut:] = recv1_ref[:, cut:] + chunk1_ref[...]
    for side, recv in enumerate((recv0_ref, far_ref)):
        edge, _ = side_of(index, side)
        rows = edge_rows(edge)
        far_rows = slice((2 + side) * BLK, (3 + side) * BLK)
        lse_own = lse_in_ref[rows, :]
        far = recv[:, 5 * feat :].astype(F32)
        scores = stack(
            [
                mm_t(q_ref[rows, head_cols(h)], recv[:, head_cols(h)]) * SCALE + mask_ref[2 + 2 * side]
                for h in range(heads)
            ]
            + [
                mm_t(recv[:, head_cols(h, 2 * feat)], k_ref[rows, head_cols(h)]) * SCALE + mask_ref[3 + 2 * side]
                for h in range(heads)
            ]
        )
        lse_part = stack(
            [lse_own[:, h : h + 1] for h in range(heads)]
            + [
                far[:, h : h + 1] + far[:, heads + h : heads + h + 1] + far[:, 2 * heads + h : 2 * heads + h + 1]
                for h in range(heads)
            ]
        )
        top = jnp.maximum(jnp.max(scores, axis=1, keepdims=True), lse_part)
        p = jnp.exp(scores - top)
        rest = jnp.exp(lse_part - top)
        total = jnp.sum(p, axis=1, keepdims=True) + rest
        lse = top + jnp.log(total)
        inv = 1.0 / total
        p = (p * inv).astype(BF16)
        rest = rest * inv
        own_stats = jnp.zeros((BLK, 128), F32)
        far_stats = jnp.zeros((BLK, 128), F32)
        sums = [jnp.zeros((BLK, HD), F32) for _ in range(4)]
        for h in range(heads):
            hs = head_cols(h)
            gain = gain_ref[:, hs]
            n = slice(h * BLK, (h + 1) * BLK)
            a = mm(p[n], recv[:, head_cols(h, feat)]) + rest[n] * o_ref[rows, hs]
            a_ref[rows, hs] = a
            own_stats = jnp.where(lane == h, lse[n], own_stats)
            sums[0] += a * a
            sums[1] += c_ref[rows, hs].astype(F32) * gain * a
            n = slice((heads + h) * BLK, (heads + h + 1) * BLK)
            a = mm(p[n], v_ref[rows, hs]) + rest[n] * recv[:, head_cols(h, 4 * feat)].astype(F32)
            a_ref[far_rows, hs] = a
            far_stats = jnp.where(lane == h, lse[n], far_stats)
            sums[2] += a * a
            sums[3] += recv[:, head_cols(h, 3 * feat)].astype(F32) * gain * a
        lse_ref[rows, :] = own_stats
        lse_ref[far_rows, :] = far_stats
        sums = [jnp.sum(x, axis=1, keepdims=True) for x in sums]
        both = jnp.where(
            lane < 2, jnp.where(lane == 0, sums[0], sums[1]), jnp.where(lane == 2, sums[2], sums[3])
        ).T
        for j in range(sums_ref.shape[0]):
            sums_ref[j, pl.ds(edge, 1), :] = both[0:1]
            sums_ref[j, pl.ds(4 + edge, 1), :] = both[1:2]
            sums_ref[j, 2 + side : 3 + side, :] = both[2:3]
            sums_ref[j, 6 + side : 7 + side, :] = both[3:4]


def grad_kernel(
    heads, mask_ref, q_ref, k_ref, v_ref, c_ref, gain_ref, a_ref, lse_ref, recv0_ref, recv1_ref, sums_ref,
    normed_ref, gq_out, gk_out, gv_out, gq_ref, gk_ref, gv_ref, d_ref, delta_ref,
):
    index = lax.axis_index("curve")
    feat = heads * HD
    gain = gain_ref[...]
    lane = lax.broadcasted_iota(jnp.int32, (BLK, 128), 1)
    total = jnp.sum(sums_ref[...], axis=0) / FEAT
    rinv = lax.rsqrt(total[0:4] + EPS)
    turn = rinv * rinv * rinv * total[4:8]
    columns = jnp.concatenate([rinv, turn, jnp.zeros((BLK - 8, 128), F32)], axis=0).T
    for b in range(4):
        rows = slice(b * BLK, (b + 1) * BLK)
        a = a_ref[rows, :]
        r, t = columns[:, b : b + 1], columns[:, 4 + b : 5 + b]
        if b < 2:
            normed_ref[rows, :] = (gain * a * r).astype(BF16)
            cot = c_ref[rows, :]
        else:
            cot = (recv0_ref, recv1_ref)[b - 2][:, 3 * feat : 4 * feat]
        d = (cot.astype(F32) * gain * r - a * t).astype(BF16)
        d_ref[rows, :] = d
        both = d.astype(F32) * a
        delta = jnp.zeros((BLK, 128), F32)
        for h in range(heads):
            delta = jnp.where(lane == h, jnp.sum(both[:, head_cols(h)], axis=1, keepdims=True), delta)
        delta_ref[rows, :] = delta
    bias = own_bias(mask_ref)
    own = slice(0, 2 * BLK)
    for h in range(heads):
        hs = head_cols(h)
        q, k, v, d = q_ref[:, hs], k_ref[:, hs], v_ref[:, hs], d_ref[own, hs]
        p = jnp.exp(mm_t(q, k) * SCALE + bias - lse_ref[own, h : h + 1])
        ds = (p * (mm_t(d, v) - delta_ref[own, h : h + 1]) * SCALE).astype(BF16)
        gq_ref[:, hs] = mm(ds, k)
        gk_ref[:, hs] = t_mm(ds, q)
        gv_ref[:, hs] = t_mm(p.astype(BF16), d)
    for side, recv in enumerate((recv0_ref, recv1_ref)):
        edge, _ = side_of(index, side)
        rows = edge_rows(edge)
        far_rows = slice((2 + side) * BLK, (3 + side) * BLK)
        pairs = [(h, q_ref[rows, head_cols(h)], recv[:, head_cols(h)], recv[:, head_cols(h, feat)], rows) for h in range(heads)]
        pairs += [
            (h, recv[:, head_cols(h, 2 * feat)], k_ref[rows, head_cols(h)], v_ref[rows, head_cols(h)], far_rows)
            for h in range(heads)
        ]
        scores = stack([mm_t(q, k) * SCALE + (mask_ref[2 + 2 * side] if n < heads else mask_ref[3 + 2 * side]) - lse_ref[r, h : h + 1] for n, (h, q, k, v, r) in enumerate(pairs)])
        dprob = stack([mm_t(d_ref[r, head_cols(h)], v) - delta_ref[r, h : h + 1] for h, q, k, v, r in pairs])
        p = jnp.exp(scores)
        ds = (p * dprob * SCALE).astype(BF16)
        p = p.astype(BF16)
        for h in range(heads):
            hs = head_cols(h)
            n = slice(h * BLK, (h + 1) * BLK)
            gq_out[rows, hs] = (gq_ref[rows, hs] + mm(ds[n], recv[:, hs])).astype(BF16)
            n = slice((heads + h) * BLK, (heads + h + 1) * BLK)
            gk_out[rows, hs] = (gk_ref[rows, hs] + t_mm(ds[n], recv[:, head_cols(h, 2 * feat)])).astype(BF16)
            gv_out[rows, hs] = (gv_ref[rows, hs] + t_mm(p[n], d_ref[far_rows, hs])).astype(BF16)


HBM = pl.BlockSpec(memory_space=pltpu.HBM)
SMEM = pl.BlockSpec(memory_space=pltpu.SMEM)
VMEM = pl.BlockSpec(memory_space=pltpu.VMEM)
PARAMS = pltpu.CompilerParams(vmem_limit_bytes=32 * 1024 * 1024)


def shape(dims, dtype):
    return jax.ShapeDtypeStruct(dims, dtype)


def call(kernel, name, in_specs, outs, scratch=(), mask_out=False):
    specs = [VMEM for _ in outs]
    if mask_out:
        specs[-1] = SMEM
    return pl.pallas_call(
        kernel,
        name=name,
        out_shape=tuple(outs),
        in_specs=in_specs,
        out_specs=tuple(specs),
        scratch_shapes=list(scratch),
        compiler_params=PARAMS,
    )


XS, YS, ZLO, CORES = 4, 8, 3, 2
AXES = ("curve", "dp")


def spot(x, y, z, core):
    return ((z // ZLO * YS + y) * XS + x) * (ZLO * CORES) + z % ZLO * CORES + core


def swaps(pairs):
    return pairs + [(b, a) for a, b in pairs]


def routes(count, peers):
    far = range(XS * YS - 1, count - 1, XS * YS)
    even = [(i * peers + j, (i + 1) * peers + j) for i in range(0, count, 2) for j in range(peers)]
    odd = [
        (i * peers + j, (i + 1) * peers + j)
        for i in range(1, count - 1, 2)
        for j in range(peers)
        if i not in far or j < CORES
    ]
    out, on = [], []
    x, y = XS - 1, YS - 1
    for block in range(len(far)):
        for part, (up, down) in ((1, ((x, 0), (0, y))), (2, ((0, 0), (x, y)))):
            for core in range(CORES):
                low, high = block * ZLO + part, (block + 1) * ZLO + part
                out += [(spot(x, y, low, core), spot(*up, low, core)), (spot(0, 0, high, core), spot(*down, high, core))]
                on += [(spot(*up, low, core), spot(0, 0, high, core)), (spot(*down, high, core), spot(x, y, low, core))]
    return swaps(even), swaps(odd), out, on


def shards(queries, keys, values, cotangent, gain, neighbour_ids, neighbour_counts):
    rows, feat = queries.shape
    heads = feat // HD
    peers = lax.axis_size("dp")
    width = 5 * feat + 128
    cut = 11 * 128
    even, odd, out, on = routes(lax.axis_size("curve"), peers)
    local = shape((rows, feat), BF16)
    send0, send1, chunk0, chunk1, o_own, lse_own, q, k, v, c, gain, mask = call(
        functools.partial(own_kernel, heads),
        "own",
        [HBM] * 7,
        [
            shape((BLK, width), BF16), shape((BLK, width), BF16), shape((BLK, cut), BF16),
            shape((BLK, width - cut), BF16), shape((rows, feat), F32), shape((rows, 128), F32),
            local, local, local, local, shape((1, feat), F32), shape((8,), F32),
        ],
        [pltpu.SMEM((NBR, BLOCKS), jnp.int32), pltpu.SMEM((BLOCKS,), jnp.int32), pltpu.SemaphoreType.DMA((7,))],
        mask_out=True,
    )(*(pltpu.with_memory_space_constraint(x, pltpu.HBM) for x in (neighbour_ids.T, neighbour_counts, queries, keys, values, cotangent, gain.reshape(1, feat))))
    chunk0 = lax.ppermute(chunk0, AXES, out)
    chunk1 = lax.ppermute(chunk1, AXES, out)
    recv1 = lax.ppermute(send1, AXES, odd)
    recv0 = lax.ppermute(send0, AXES, even)
    chunk0 = lax.ppermute(chunk0, AXES, on)
    chunk1 = lax.ppermute(chunk1, AXES, on)
    attended, lse, sums, recv1 = call(
        functools.partial(join_kernel, heads),
        "join",
        [SMEM] + [VMEM] * 11,
        [
            shape((2 * rows, feat), F32), shape((2 * rows, 128), F32), shape((peers, 8, 128), F32),
            shape((BLK, width), BF16),
        ],
    )(mask, q, k, v, c, gain, o_own, lse_own, recv0, recv1, chunk0, chunk1)
    sums = lax.all_to_all(sums, "dp", 0, 0, tiled=True)
    return call(
        functools.partial(grad_kernel, heads),
        "grads",
        [SMEM] + [VMEM] * 10,
        [local] * 4,
        [pltpu.VMEM((rows, feat), F32)] * 3 + [pltpu.VMEM((2 * rows, feat), BF16), pltpu.VMEM((2 * rows, 128), F32)],
    )(mask, q, k, v, c, gain, attended, lse, recv0, recv1, sums)


def solution(mesh):
    wide = P("curve", "dp")
    return jax.shard_map(
        shards,
        mesh=mesh,
        in_specs=(wide, wide, wide, wide, P("dp"), P(), P()),
        out_specs=(wide, wide, wide, wide),
        check_vma=False,
    )
```

```python
import functools
import math

import jax
import jax.numpy as jnp
from jax import lax
from jax.experimental import pallas as pl
from jax.experimental.pallas import tpu as pltpu
from jax.sharding import PartitionSpec as P

FEAT = 3072
HD = 128
BLK = 128
NBR = 3
BLOCKS = 256
EPS = 1e-06
SCALE = 1.0 / math.sqrt(HD)
NEG = -1e30
F32 = jnp.float32
BF16 = jnp.bfloat16


def mm(a, b):
    return lax.dot_general(a, b, (((1,), (0,)), ((), ())), preferred_element_type=F32)


def mm_t(a, b):
    return lax.dot_general(a, b, (((1,), (1,)), ((), ())), preferred_element_type=F32)


def t_mm(a, b):
    return lax.dot_general(a, b, (((0,), (0,)), ((), ())), preferred_element_type=F32)


def sees(ids_ref, cnt_ref, a, b):
    inside = jnp.logical_and(a >= 0, a < BLOCKS)
    row = jnp.clip(a, 0, BLOCKS - 1)
    hit = jnp.bool_(False)
    for j in range(NBR):
        hit = jnp.logical_or(hit, jnp.logical_and(j < cnt_ref[row], ids_ref[j, row] == b))
    return jnp.where(jnp.logical_and(hit, inside), F32(0.0), F32(NEG))


def own_bias(mask_ref):
    row = lax.broadcasted_iota(jnp.int32, (2 * BLK, 2 * BLK), 0) >= BLK
    col = lax.broadcasted_iota(jnp.int32, (2 * BLK, 2 * BLK), 1) >= BLK
    off = jnp.where(row, mask_ref[1], mask_ref[0])
    return jnp.where(row == col, F32(0.0), off)


def side_of(index, side):
    even = 1 - lax.rem(index, 2)
    edge = even if side == 0 else 1 - even
    return edge, 2 * edge - 1


def edge_rows(edge):
    return pl.ds(pl.multiple_of(edge * BLK, BLK), BLK)


def head_cols(h, base=0):
    return slice(base + h * HD, base + (h + 1) * HD)


def own_kernel(
    heads, ids_hbm, cnt_hbm, q_hbm, k_hbm, v_hbm, c_hbm, gain_hbm,
    send1_ref, send0_ref, chunk0_ref, chunk1_ref, o_ref, lse_ref, q_ref, k_ref, v_ref, c_ref, gain_ref, mask_ref,
    ids_ref, cnt_ref, sems,
):
    index = lax.axis_index("curve")
    feat = heads * HD
    copies = [
        pltpu.make_async_copy(src, dst, sems.at[n])
        for n, (src, dst) in enumerate(
            (
                (ids_hbm, ids_ref), (cnt_hbm, cnt_ref), (q_hbm, q_ref), (k_hbm, k_ref), (v_hbm, v_ref),
                (c_hbm, c_ref), (gain_hbm, gain_ref),
            )
        )
    ]
    for copy in copies:
        copy.start()
    for copy in copies[:2]:
        copy.wait()
    first = 2 * index
    mask_ref[0] = sees(ids_ref, cnt_ref, first, first + 1)
    mask_ref[1] = sees(ids_ref, cnt_ref, first + 1, first)
    for side in range(2):
        edge, step = side_of(index, side)
        block = first + edge
        mask_ref[2 + 2 * side] = sees(ids_ref, cnt_ref, block, block + step)
        mask_ref[3 + 2 * side] = sees(ids_ref, cnt_ref, block + step, block)
    bias = own_bias(mask_ref)
    for copy in copies[2:]:
        copy.wait()
    lane = lax.broadcasted_iota(jnp.int32, (2 * BLK, 128), 1)
    stats = jnp.zeros((2 * BLK, 128), F32)
    for h in range(heads):
        hs = head_cols(h)
        s = mm_t(q_ref[:, hs], k_ref[:, hs]) * SCALE + bias
        top = jnp.max(s, axis=1, keepdims=True)
        p = jnp.exp(s - top)
        total = jnp.sum(p, axis=1, keepdims=True)
        o_ref[:, hs] = mm(p.astype(BF16), v_ref[:, hs]) / total
        stats = jnp.where(lax.rem(lane, heads) == h, top + jnp.log(total), stats)
    lse_ref[...] = stats
    for side, send in enumerate((send0_ref, send1_ref)):
        edge, _ = side_of(index, side)
        rows = edge_rows(edge)
        for n, ref in enumerate((k_ref, v_ref, q_ref, c_ref)):
            send[:, n * feat : (n + 1) * feat] = ref[rows, :]
        send[:, 4 * feat : 5 * feat] = o_ref[rows, :].astype(BF16)
        lse = lse_ref[rows, :]
        lane = lax.broadcasted_iota(jnp.int32, (BLK, 128), 1)
        hi = lse.astype(BF16).astype(F32)
        mid = (lse - hi).astype(BF16).astype(F32)
        parts = jnp.where(lane < heads, hi, jnp.where(lane < 2 * heads, mid, lse - hi - mid))
        send[:, 5 * feat :] = parts.astype(BF16)
    cut = chunk0_ref.shape[1]
    chunk0_ref[...] = send1_ref[:, :cut]
    chunk1_ref[...] = send1_ref[:, -cut:]


def stack(parts):
    return jnp.concatenate(parts, axis=0)


def join_kernel(
    heads, mask_ref, q_ref, k_ref, v_ref, c_ref, gain_ref, o_ref, lse_in_ref, recv0_ref, recv1_ref, chunk0_ref,
    chunk1_ref, a_ref, lse_ref, sums_ref, far_ref,
):
    index = lax.axis_index("curve")
    feat = heads * HD
    cut = chunk0_ref.shape[1]
    lane = lax.broadcasted_iota(jnp.int32, (BLK, 128), 1)
    far_ref[:, :cut] = recv1_ref[:, :cut] + chunk0_ref[...]
    far_ref[:, cut:] = recv1_ref[:, cut:] + chunk1_ref[:, 2 * cut - recv1_ref.shape[1] :]
    for side, recv in enumerate((recv0_ref, far_ref)):
        edge, _ = side_of(index, side)
        rows = edge_rows(edge)
        far_rows = slice((2 + side) * BLK, (3 + side) * BLK)
        lse_own = lse_in_ref[rows, :]
        far = recv[:, 5 * feat :].astype(F32)
        scores = stack(
            [
                mm_t(q_ref[rows, head_cols(h)], recv[:, head_cols(h)]) * SCALE + mask_ref[2 + 2 * side]
                for h in range(heads)
            ]
            + [
                mm_t(recv[:, head_cols(h, 2 * feat)], k_ref[rows, head_cols(h)]) * SCALE + mask_ref[3 + 2 * side]
                for h in range(heads)
            ]
        )
        lse_part = stack(
            [lse_own[:, h : h + 1] for h in range(heads)]
            + [
                far[:, h : h + 1] + far[:, heads + h : heads + h + 1] + far[:, 2 * heads + h : 2 * heads + h + 1]
                for h in range(heads)
            ]
        )
        top = jnp.maximum(jnp.max(scores, axis=1, keepdims=True), lse_part)
        p = jnp.exp(scores - top)
        rest = jnp.exp(lse_part - top)
        total = jnp.sum(p, axis=1, keepdims=True) + rest
        lse = top + jnp.log(total)
        inv = 1.0 / total
        p = (p * inv).astype(BF16)
        rest = rest * inv
        own_stats = jnp.zeros((BLK, 128), F32)
        far_stats = jnp.zeros((BLK, 128), F32)
        sums = [jnp.zeros((BLK, HD), F32) for _ in range(4)]
        for h in range(heads):
            hs = head_cols(h)
            gain = gain_ref[:, hs]
            n = slice(h * BLK, (h + 1) * BLK)
            a = mm(p[n], recv[:, head_cols(h, feat)]) + rest[n] * o_ref[rows, hs]
            a_ref[rows, hs] = a
            own_stats = jnp.where(lane == h, lse[n], own_stats)
            sums[0] += a * a
            sums[1] += c_ref[rows, hs].astype(F32) * gain * a
            n = slice((heads + h) * BLK, (heads + h + 1) * BLK)
            a = mm(p[n], v_ref[rows, hs]) + rest[n] * recv[:, head_cols(h, 4 * feat)].astype(F32)
            a_ref[far_rows, hs] = a
            far_stats = jnp.where(lane == h, lse[n], far_stats)
            sums[2] += a * a
            sums[3] += recv[:, head_cols(h, 3 * feat)].astype(F32) * gain * a
        lse_ref[rows, :] = own_stats
        lse_ref[far_rows, :] = far_stats
        sums = [jnp.sum(x, axis=1, keepdims=True) for x in sums]
        both = jnp.where(
            lane < 2, jnp.where(lane == 0, sums[0], sums[1]), jnp.where(lane == 2, sums[2], sums[3])
        ).T
        for j in range(sums_ref.shape[0]):
            sums_ref[j, pl.ds(edge, 1), :] = both[0:1]
            sums_ref[j, pl.ds(4 + edge, 1), :] = both[1:2]
            sums_ref[j, 2 + side : 3 + side, :] = both[2:3]
            sums_ref[j, 6 + side : 7 + side, :] = both[3:4]


def grad_kernel(
    heads, mask_ref, q_ref, k_ref, v_ref, c_ref, gain_ref, a_ref, lse_ref, recv0_ref, recv1_ref, sums_ref,
    normed_ref, gq_out, gk_out, gv_out, gq_ref, gk_ref, gv_ref, d_ref, delta_ref,
):
    index = lax.axis_index("curve")
    feat = heads * HD
    gain = gain_ref[...]
    lane = lax.broadcasted_iota(jnp.int32, (BLK, 128), 1)
    total = jnp.sum(sums_ref[...], axis=0) / FEAT
    rinv = lax.rsqrt(total[0:4] + EPS)
    turn = rinv * rinv * rinv * total[4:8]
    columns = jnp.concatenate([rinv, turn, jnp.zeros((BLK - 8, 128), F32)], axis=0).T
    for b in range(4):
        rows = slice(b * BLK, (b + 1) * BLK)
        a = a_ref[rows, :]
        r, t = columns[:, b : b + 1], columns[:, 4 + b : 5 + b]
        if b < 2:
            normed_ref[rows, :] = (gain * a * r).astype(BF16)
            cot = c_ref[rows, :]
        else:
            cot = (recv0_ref, recv1_ref)[b - 2][:, 3 * feat : 4 * feat]
        d = (cot.astype(F32) * gain * r - a * t).astype(BF16)
        d_ref[rows, :] = d
        both = d.astype(F32) * a
        delta = jnp.zeros((BLK, 128), F32)
        for h in range(heads):
            delta = jnp.where(lane == h, jnp.sum(both[:, head_cols(h)], axis=1, keepdims=True), delta)
        delta_ref[rows, :] = delta
    bias = own_bias(mask_ref)
    own = slice(0, 2 * BLK)
    for h in range(heads):
        hs = head_cols(h)
        q, k, v, d = q_ref[:, hs], k_ref[:, hs], v_ref[:, hs], d_ref[own, hs]
        p = jnp.exp(mm_t(q, k) * SCALE + bias - lse_ref[own, h : h + 1])
        ds = (p * (mm_t(d, v) - delta_ref[own, h : h + 1]) * SCALE).astype(BF16)
        gq_ref[:, hs] = mm(ds, k)
        gk_ref[:, hs] = t_mm(ds, q)
        gv_ref[:, hs] = t_mm(p.astype(BF16), d)
    for side, recv in enumerate((recv0_ref, recv1_ref)):
        edge, _ = side_of(index, side)
        rows = edge_rows(edge)
        far_rows = slice((2 + side) * BLK, (3 + side) * BLK)
        pairs = [(h, q_ref[rows, head_cols(h)], recv[:, head_cols(h)], recv[:, head_cols(h, feat)], rows) for h in range(heads)]
        pairs += [
            (h, recv[:, head_cols(h, 2 * feat)], k_ref[rows, head_cols(h)], v_ref[rows, head_cols(h)], far_rows)
            for h in range(heads)
        ]
        scores = stack([mm_t(q, k) * SCALE + (mask_ref[2 + 2 * side] if n < heads else mask_ref[3 + 2 * side]) - lse_ref[r, h : h + 1] for n, (h, q, k, v, r) in enumerate(pairs)])
        dprob = stack([mm_t(d_ref[r, head_cols(h)], v) - delta_ref[r, h : h + 1] for h, q, k, v, r in pairs])
        p = jnp.exp(scores)
        ds = (p * dprob * SCALE).astype(BF16)
        p = p.astype(BF16)
        for h in range(heads):
            hs = head_cols(h)
            n = slice(h * BLK, (h + 1) * BLK)
            gq_out[rows, hs] = (gq_ref[rows, hs] + mm(ds[n], recv[:, hs])).astype(BF16)
            n = slice((heads + h) * BLK, (heads + h + 1) * BLK)
            gk_out[rows, hs] = (gk_ref[rows, hs] + t_mm(ds[n], recv[:, head_cols(h, 2 * feat)])).astype(BF16)
            gv_out[rows, hs] = (gv_ref[rows, hs] + t_mm(p[n], d_ref[far_rows, hs])).astype(BF16)


HBM = pl.BlockSpec(memory_space=pltpu.HBM)
SMEM = pl.BlockSpec(memory_space=pltpu.SMEM)
VMEM = pl.BlockSpec(memory_space=pltpu.VMEM)
PARAMS = pltpu.CompilerParams(vmem_limit_bytes=32 * 1024 * 1024)


def shape(dims, dtype):
    return jax.ShapeDtypeStruct(dims, dtype)


def call(kernel, name, in_specs, outs, scratch=(), mask_out=False):
    specs = [VMEM for _ in outs]
    if mask_out:
        specs[-1] = SMEM
    return pl.pallas_call(
        kernel,
        name=name,
        out_shape=tuple(outs),
        in_specs=in_specs,
        out_specs=tuple(specs),
        scratch_shapes=list(scratch),
        compiler_params=PARAMS,
    )


XS, YS, ZLO, CORES = 4, 8, 3, 2
AXES = ("curve", "dp")


def spot(x, y, z, core):
    return ((z // ZLO * YS + y) * XS + x) * (ZLO * CORES) + z % ZLO * CORES + core


def swaps(pairs):
    return pairs + [(b, a) for a, b in pairs]


def routes(count, peers):
    far = range(XS * YS - 1, count - 1, XS * YS)
    even = [(i * peers + j, (i + 1) * peers + j) for i in range(0, count, 2) for j in range(peers)]
    odd = [
        (i * peers + j, (i + 1) * peers + j)
        for i in range(1, count - 1, 2)
        for j in range(peers)
        if i not in far or j >= (ZLO - 1) * CORES
    ]
    out, on = [], []
    x, y = XS - 1, YS - 1
    for block in range(len(far)):
        for part, (up, down) in ((0, ((x, y - 1), (0, 1))), (1, ((x, 0), (0, y)))):
            for core in range(CORES):
                low, high = block * ZLO + part, (block + 1) * ZLO + part
                out += [(spot(x, y, low, core), spot(*up, low, core)), (spot(0, 0, high, core), spot(*down, high, core))]
                on += [(spot(*up, low, core), spot(0, 0, high, core)), (spot(*down, high, core), spot(x, y, low, core))]
    return swaps(even), swaps(odd), out, on


def shards(queries, keys, values, cotangent, gain, neighbour_ids, neighbour_counts):
    rows, feat = queries.shape
    heads = feat // HD
    peers = lax.axis_size("dp")
    width = 5 * feat + 128
    cut = 11 * 128
    even, odd, out, on = routes(lax.axis_size("curve"), peers)
    local = shape((rows, feat), BF16)
    send1, send0, chunk0, chunk1, o_own, lse_own, q, k, v, c, gain, mask = call(
        functools.partial(own_kernel, heads),
        "own",
        [HBM] * 7,
        [
            shape((BLK, width), BF16), shape((BLK, width), BF16), shape((BLK, cut), BF16),
            shape((BLK, cut), BF16), shape((rows, feat), F32), shape((rows, 128), F32),
            local, local, local, local, shape((1, feat), F32), shape((8,), F32),
        ],
        [pltpu.SMEM((NBR, BLOCKS), jnp.int32), pltpu.SMEM((BLOCKS,), jnp.int32), pltpu.SemaphoreType.DMA((7,))],
        mask_out=True,
    )(*(pltpu.with_memory_space_constraint(x, pltpu.HBM) for x in (neighbour_ids.T, neighbour_counts, queries, keys, values, cotangent, gain.reshape(1, feat))))
    chunk0 = lax.ppermute(chunk0, AXES, out)
    chunk1 = lax.ppermute(chunk1, AXES, out)
    recv1 = lax.ppermute(send1, AXES, odd)
    recv0 = lax.ppermute(send0, AXES, even)
    chunk0 = lax.ppermute(chunk0, AXES, on)
    chunk1 = lax.ppermute(chunk1, AXES, on)
    attended, lse, sums, recv1 = call(
        functools.partial(join_kernel, heads),
        "join",
        [SMEM] + [VMEM] * 11,
        [
            shape((2 * rows, feat), F32), shape((2 * rows, 128), F32), shape((peers, 8, 128), F32),
            shape((BLK, width), BF16),
        ],
    )(mask, q, k, v, c, gain, o_own, lse_own, recv0, recv1, chunk0, chunk1)
    sums = lax.all_to_all(sums, "dp", 0, 0, tiled=True)
    return call(
        functools.partial(grad_kernel, heads),
        "grads",
        [SMEM] + [VMEM] * 10,
        [local] * 4,
        [pltpu.VMEM((rows, feat), F32)] * 3 + [pltpu.VMEM((2 * rows, feat), BF16), pltpu.VMEM((2 * rows, 128), F32)],
    )(mask, q, k, v, c, gain, attended, lse, recv0, recv1, sums)


def solution(mesh):
    wide = P("curve", "dp")
    return jax.shard_map(
        shards,
        mesh=mesh,
        in_specs=(wide, wide, wide, wide, P("dp"), P(), P()),
        out_specs=(wide, wide, wide, wide),
        check_vma=False,
    )
```

```python
import functools
import math

import jax
import jax.numpy as jnp
from jax import lax
from jax.experimental import pallas as pl
from jax.experimental.pallas import tpu as pltpu
from jax.sharding import PartitionSpec as P

FEAT = 3072
HD = 128
BLK = 128
NBR = 3
BLOCKS = 256
EPS = 1e-06
SCALE = 1.0 / math.sqrt(HD)
NEG = -1e30
F32 = jnp.float32
BF16 = jnp.bfloat16


def mm(a, b):
    return lax.dot_general(a, b, (((1,), (0,)), ((), ())), preferred_element_type=F32)


def mm_t(a, b):
    return lax.dot_general(a, b, (((1,), (1,)), ((), ())), preferred_element_type=F32)


def t_mm(a, b):
    return lax.dot_general(a, b, (((0,), (0,)), ((), ())), preferred_element_type=F32)


def sees(ids_ref, cnt_ref, a, b):
    inside = jnp.logical_and(a >= 0, a < BLOCKS)
    row = jnp.clip(a, 0, BLOCKS - 1)
    hit = jnp.bool_(False)
    for j in range(NBR):
        hit = jnp.logical_or(hit, jnp.logical_and(j < cnt_ref[row], ids_ref[j, row] == b))
    return jnp.where(jnp.logical_and(hit, inside), F32(0.0), F32(NEG))


def own_bias(mask_ref):
    row = lax.broadcasted_iota(jnp.int32, (2 * BLK, 2 * BLK), 0) >= BLK
    col = lax.broadcasted_iota(jnp.int32, (2 * BLK, 2 * BLK), 1) >= BLK
    off = jnp.where(row, mask_ref[1], mask_ref[0])
    return jnp.where(row == col, F32(0.0), off)


def side_of(index, side):
    even = 1 - lax.rem(index, 2)
    edge = even if side == 0 else 1 - even
    return edge, 2 * edge - 1


def edge_rows(edge):
    return pl.ds(pl.multiple_of(edge * BLK, BLK), BLK)


def head_cols(h, base=0):
    return slice(base + h * HD, base + (h + 1) * HD)


def own_kernel(
    heads, ids_hbm, cnt_hbm, q_hbm, k_hbm, v_hbm, c_hbm, gain_hbm,
    send1_ref, send0_ref, o_ref, lse_ref, q_ref, k_ref, v_ref, c_ref, gain_ref, mask_ref, *rest,
):
    *chunk_refs, ids_ref, cnt_ref, sems = rest
    index = lax.axis_index("curve")
    feat = heads * HD
    copies = [
        pltpu.make_async_copy(src, dst, sems.at[n])
        for n, (src, dst) in enumerate(
            (
                (ids_hbm, ids_ref), (cnt_hbm, cnt_ref), (q_hbm, q_ref), (k_hbm, k_ref), (v_hbm, v_ref),
                (c_hbm, c_ref), (gain_hbm, gain_ref),
            )
        )
    ]
    for copy in copies:
        copy.start()
    for copy in copies[:2]:
        copy.wait()
    first = 2 * index
    mask_ref[0] = sees(ids_ref, cnt_ref, first, first + 1)
    mask_ref[1] = sees(ids_ref, cnt_ref, first + 1, first)
    for side in range(2):
        edge, step = side_of(index, side)
        block = first + edge
        mask_ref[2 + 2 * side] = sees(ids_ref, cnt_ref, block, block + step)
        mask_ref[3 + 2 * side] = sees(ids_ref, cnt_ref, block + step, block)
    bias = own_bias(mask_ref)
    for copy in copies[2:]:
        copy.wait()
    lane = lax.broadcasted_iota(jnp.int32, (2 * BLK, 128), 1)
    stats = jnp.zeros((2 * BLK, 128), F32)
    for h in range(heads):
        hs = head_cols(h)
        s = mm_t(q_ref[:, hs], k_ref[:, hs]) * SCALE + bias
        top = jnp.max(s, axis=1, keepdims=True)
        p = jnp.exp(s - top)
        total = jnp.sum(p, axis=1, keepdims=True)
        o_ref[:, hs] = mm(p.astype(BF16), v_ref[:, hs]) / total
        stats = jnp.where(lax.rem(lane, heads) == h, top + jnp.log(total), stats)
    lse_ref[...] = stats
    for side, send in enumerate((send0_ref, send1_ref)):
        edge, _ = side_of(index, side)
        rows = edge_rows(edge)
        for n, ref in enumerate((k_ref, v_ref, q_ref, c_ref)):
            send[:, n * feat : (n + 1) * feat] = ref[rows, :]
        send[:, 4 * feat : 5 * feat] = o_ref[rows, :].astype(BF16)
        lse = lse_ref[rows, :]
        lane = lax.broadcasted_iota(jnp.int32, (BLK, 128), 1)
        hi = lse.astype(BF16).astype(F32)
        mid = (lse - hi).astype(BF16).astype(F32)
        parts = jnp.where(lane < heads, hi, jnp.where(lane < 2 * heads, mid, lse - hi - mid))
        send[:, 5 * feat :] = parts.astype(BF16)
    cut = chunk_refs[0].shape[1]
    for n, chunk in enumerate(chunk_refs):
        chunk[...] = send1_ref[:, n * cut : (n + 1) * cut]


def stack(parts):
    return jnp.concatenate(parts, axis=0)


def merge_kernel(*refs):
    *chunk_refs, out_ref = refs
    cut = chunk_refs[0].shape[1]
    for n, chunk in enumerate(chunk_refs):
        out_ref[:, n * cut : (n + 1) * cut] = chunk[...]


def add_kernel(a_ref, b_ref, out_ref):
    out_ref[...] = a_ref[...] + b_ref[...]


def join_kernel(
    heads, mask_ref, q_ref, k_ref, v_ref, c_ref, gain_ref, o_ref, lse_in_ref, recv0_ref, recv1_ref,
    a_ref, lse_ref, sums_ref,
):
    index = lax.axis_index("curve")
    feat = heads * HD
    lane = lax.broadcasted_iota(jnp.int32, (BLK, 128), 1)
    for side, recv in enumerate((recv0_ref, recv1_ref)):
        edge, _ = side_of(index, side)
        rows = edge_rows(edge)
        far_rows = slice((2 + side) * BLK, (3 + side) * BLK)
        lse_own = lse_in_ref[rows, :]
        far = recv[:, 5 * feat :].astype(F32)
        scores = stack(
            [
                mm_t(q_ref[rows, head_cols(h)], recv[:, head_cols(h)]) * SCALE + mask_ref[2 + 2 * side]
                for h in range(heads)
            ]
            + [
                mm_t(recv[:, head_cols(h, 2 * feat)], k_ref[rows, head_cols(h)]) * SCALE + mask_ref[3 + 2 * side]
                for h in range(heads)
            ]
        )
        lse_part = stack(
            [lse_own[:, h : h + 1] for h in range(heads)]
            + [
                far[:, h : h + 1] + far[:, heads + h : heads + h + 1] + far[:, 2 * heads + h : 2 * heads + h + 1]
                for h in range(heads)
            ]
        )
        top = jnp.maximum(jnp.max(scores, axis=1, keepdims=True), lse_part)
        p = jnp.exp(scores - top)
        rest = jnp.exp(lse_part - top)
        total = jnp.sum(p, axis=1, keepdims=True) + rest
        lse = top + jnp.log(total)
        inv = 1.0 / total
        p = (p * inv).astype(BF16)
        rest = rest * inv
        own_stats = jnp.zeros((BLK, 128), F32)
        far_stats = jnp.zeros((BLK, 128), F32)
        sums = [jnp.zeros((BLK, HD), F32) for _ in range(4)]
        for h in range(heads):
            hs = head_cols(h)
            gain = gain_ref[:, hs]
            n = slice(h * BLK, (h + 1) * BLK)
            a = mm(p[n], recv[:, head_cols(h, feat)]) + rest[n] * o_ref[rows, hs]
            a_ref[rows, hs] = a
            own_stats = jnp.where(lane == h, lse[n], own_stats)
            sums[0] += a * a
            sums[1] += c_ref[rows, hs].astype(F32) * gain * a
            n = slice((heads + h) * BLK, (heads + h + 1) * BLK)
            a = mm(p[n], v_ref[rows, hs]) + rest[n] * recv[:, head_cols(h, 4 * feat)].astype(F32)
            a_ref[far_rows, hs] = a
            far_stats = jnp.where(lane == h, lse[n], far_stats)
            sums[2] += a * a
            sums[3] += recv[:, head_cols(h, 3 * feat)].astype(F32) * gain * a
        lse_ref[rows, :] = own_stats
        lse_ref[far_rows, :] = far_stats
        sums = [jnp.sum(x, axis=1, keepdims=True) for x in sums]
        both = jnp.where(
            lane < 2, jnp.where(lane == 0, sums[0], sums[1]), jnp.where(lane == 2, sums[2], sums[3])
        ).T
        for j in range(sums_ref.shape[0]):
            sums_ref[j, pl.ds(edge, 1), :] = both[0:1]
            sums_ref[j, pl.ds(4 + edge, 1), :] = both[1:2]
            sums_ref[j, 2 + side : 3 + side, :] = both[2:3]
            sums_ref[j, 6 + side : 7 + side, :] = both[3:4]


def grad_kernel(
    heads, mask_ref, q_ref, k_ref, v_ref, c_ref, gain_ref, a_ref, lse_ref, recv0_ref, recv1_ref, sums_ref,
    normed_ref, gq_out, gk_out, gv_out, gq_ref, gk_ref, gv_ref, d_ref, delta_ref,
):
    index = lax.axis_index("curve")
    feat = heads * HD
    gain = gain_ref[...]
    lane = lax.broadcasted_iota(jnp.int32, (BLK, 128), 1)
    total = jnp.sum(sums_ref[...], axis=0) / FEAT
    rinv = lax.rsqrt(total[0:4] + EPS)
    turn = rinv * rinv * rinv * total[4:8]
    columns = jnp.concatenate([rinv, turn, jnp.zeros((BLK - 8, 128), F32)], axis=0).T
    for b in range(4):
        rows = slice(b * BLK, (b + 1) * BLK)
        a = a_ref[rows, :]
        r, t = columns[:, b : b + 1], columns[:, 4 + b : 5 + b]
        if b < 2:
            normed_ref[rows, :] = (gain * a * r).astype(BF16)
            cot = c_ref[rows, :]
        else:
            cot = (recv0_ref, recv1_ref)[b - 2][:, 3 * feat : 4 * feat]
        d = (cot.astype(F32) * gain * r - a * t).astype(BF16)
        d_ref[rows, :] = d
        both = d.astype(F32) * a
        delta = jnp.zeros((BLK, 128), F32)
        for h in range(heads):
            delta = jnp.where(lane == h, jnp.sum(both[:, head_cols(h)], axis=1, keepdims=True), delta)
        delta_ref[rows, :] = delta
    bias = own_bias(mask_ref)
    own = slice(0, 2 * BLK)
    for h in range(heads):
        hs = head_cols(h)
        q, k, v, d = q_ref[:, hs], k_ref[:, hs], v_ref[:, hs], d_ref[own, hs]
        p = jnp.exp(mm_t(q, k) * SCALE + bias - lse_ref[own, h : h + 1])
        ds = (p * (mm_t(d, v) - delta_ref[own, h : h + 1]) * SCALE).astype(BF16)
        gq_ref[:, hs] = mm(ds, k)
        gk_ref[:, hs] = t_mm(ds, q)
        gv_ref[:, hs] = t_mm(p.astype(BF16), d)
    for side, recv in enumerate((recv0_ref, recv1_ref)):
        edge, _ = side_of(index, side)
        rows = edge_rows(edge)
        far_rows = slice((2 + side) * BLK, (3 + side) * BLK)
        pairs = [(h, q_ref[rows, head_cols(h)], recv[:, head_cols(h)], recv[:, head_cols(h, feat)], rows) for h in range(heads)]
        pairs += [
            (h, recv[:, head_cols(h, 2 * feat)], k_ref[rows, head_cols(h)], v_ref[rows, head_cols(h)], far_rows)
            for h in range(heads)
        ]
        scores = stack([mm_t(q, k) * SCALE + (mask_ref[2 + 2 * side] if n < heads else mask_ref[3 + 2 * side]) - lse_ref[r, h : h + 1] for n, (h, q, k, v, r) in enumerate(pairs)])
        dprob = stack([mm_t(d_ref[r, head_cols(h)], v) - delta_ref[r, h : h + 1] for h, q, k, v, r in pairs])
        p = jnp.exp(scores)
        ds = (p * dprob * SCALE).astype(BF16)
        p = p.astype(BF16)
        for h in range(heads):
            hs = head_cols(h)
            n = slice(h * BLK, (h + 1) * BLK)
            gq_out[rows, hs] = (gq_ref[rows, hs] + mm(ds[n], recv[:, hs])).astype(BF16)
            n = slice((heads + h) * BLK, (heads + h + 1) * BLK)
            gk_out[rows, hs] = (gk_ref[rows, hs] + t_mm(ds[n], recv[:, head_cols(h, 2 * feat)])).astype(BF16)
            gv_out[rows, hs] = (gv_ref[rows, hs] + t_mm(p[n], d_ref[far_rows, hs])).astype(BF16)


HBM = pl.BlockSpec(memory_space=pltpu.HBM)
SMEM = pl.BlockSpec(memory_space=pltpu.SMEM)
VMEM = pl.BlockSpec(memory_space=pltpu.VMEM)
PARAMS = pltpu.CompilerParams(vmem_limit_bytes=32 * 1024 * 1024)


def shape(dims, dtype):
    return jax.ShapeDtypeStruct(dims, dtype)


def call(kernel, name, in_specs, outs, scratch=(), mask_out=None, cost=None):
    specs = [VMEM for _ in outs]
    if mask_out is not None:
        specs[mask_out] = SMEM
    return pl.pallas_call(
        kernel,
        name=name,
        out_shape=tuple(outs),
        in_specs=in_specs,
        out_specs=tuple(specs),
        scratch_shapes=list(scratch),
        compiler_params=PARAMS,
        cost_estimate=cost,
    )


XS, YS, ZLO, CORES = 4, 8, 3, 2
AXES = ("curve", "dp")


def spot(x, y, z, core):
    return ((z // ZLO * YS + y) * XS + x) * (ZLO * CORES) + z % ZLO * CORES + core


def swaps(pairs):
    return pairs + [(b, a) for a, b in pairs]


BESIDE, BEYOND, ACROSS = ((3, 6), (0, 1)), ((2, 6), (1, 1)), ((3, 0), (0, 7))
RELAYS = ((BESIDE, BESIDE, BEYOND), (ACROSS, ACROSS, ACROSS))
CHUNKS = 3


def routes(count, peers):
    far = range(XS * YS - 1, count - 1, XS * YS)
    even = [(i * peers + j, (i + 1) * peers + j) for i in range(0, count, 2) for j in range(peers)]
    odd = [
        (i * peers + j, (i + 1) * peers + j)
        for i in range(1, count - 1, 2)
        for j in range(peers)
        if i not in far or j >= len(RELAYS) * CORES
    ]
    hops = []
    for chunk in range(CHUNKS):
        out, on = [], []
        for block in range(len(far)):
            for part, relays in enumerate(RELAYS):
                up, down = relays[chunk]
                low, high = block * ZLO + part, (block + 1) * ZLO + part
                for core in range(CORES):
                    first, last = spot(XS - 1, YS - 1, low, core), spot(0, 0, high, core)
                    over, back = spot(*up, low, core), spot(*down, high, core)
                    out += [(first, over), (last, back)]
                    on += [(over, last), (back, first)]
        hops.append((out, on))
    return swaps(even), swaps(odd), hops


def shards(queries, keys, values, cotangent, gain, neighbour_ids, neighbour_counts):
    rows, feat = queries.shape
    heads = feat // HD
    peers = lax.axis_size("dp")
    width = 5 * feat + 128
    cut = width // CHUNKS
    even, odd, hops = routes(lax.axis_size("curve"), peers)
    local = shape((rows, feat), BF16)
    send1, send0, o_own, lse_own, q, k, v, c, gain, mask, *chunks = call(
        functools.partial(own_kernel, heads),
        "own",
        [HBM] * 7,
        [
            shape((BLK, width), BF16), shape((BLK, width), BF16), shape((rows, feat), F32), shape((rows, 128), F32),
            local, local, local, local, shape((1, feat), F32), shape((8,), F32),
        ]
        + [shape((BLK, cut), BF16)] * CHUNKS,
        [pltpu.SMEM((NBR, BLOCKS), jnp.int32), pltpu.SMEM((BLOCKS,), jnp.int32), pltpu.SemaphoreType.DMA((7,))],
        mask_out=9,
    )(*(pltpu.with_memory_space_constraint(x, pltpu.HBM) for x in (neighbour_ids.T, neighbour_counts, queries, keys, values, cotangent, gain.reshape(1, feat))))
    chunks = [lax.ppermute(chunk, AXES, out) for chunk, (out, _) in zip(chunks, hops)]
    recv1 = lax.ppermute(send1, AXES, odd)
    recv0 = lax.ppermute(send0, AXES, even)
    chunks = [lax.ppermute(chunk, AXES, on) for chunk, (_, on) in zip(chunks, hops)]
    (relayed,) = call(
        merge_kernel, "merge", [VMEM] * CHUNKS, [shape((BLK, width), BF16)],
        cost=pl.CostEstimate(flops=4 * 10**9, bytes_accessed=4 * BLK * width, transcendentals=0),
    )(*chunks)
    (recv1,) = call(add_kernel, "odd", [VMEM] * 2, [shape((BLK, width), BF16)])(recv1, relayed)
    attended, lse, sums = call(
        functools.partial(join_kernel, heads),
        "join",
        [SMEM] + [VMEM] * 9,
        [
            shape((2 * rows, feat), F32), shape((2 * rows, 128), F32), shape((peers, 8, 128), F32),
        ],
    )(mask, q, k, v, c, gain, o_own, lse_own, recv0, recv1)
    sums = lax.all_to_all(sums, "dp", 0, 0, tiled=True)
    return call(
        functools.partial(grad_kernel, heads),
        "grads",
        [SMEM] + [VMEM] * 10,
        [local] * 4,
        [pltpu.VMEM((rows, feat), F32)] * 3 + [pltpu.VMEM((2 * rows, feat), BF16), pltpu.VMEM((2 * rows, 128), F32)],
    )(mask, q, k, v, c, gain, attended, lse, recv0, recv1, sums)


def solution(mesh):
    wide = P("curve", "dp")
    return jax.shard_map(
        shards,
        mesh=mesh,
        in_specs=(wide, wide, wide, wide, P("dp"), P(), P()),
        out_specs=(wide, wide, wide, wide),
        check_vma=False,
    )
```

```python
import functools
import math

import jax
import jax.numpy as jnp
from jax import lax
from jax.experimental import pallas as pl
from jax.experimental.pallas import tpu as pltpu
from jax.sharding import PartitionSpec as P

FEAT = 3072
HD = 128
BLK = 128
NBR = 3
BLOCKS = 256
EPS = 1e-06
SCALE = 1.0 / math.sqrt(HD)
NEG = -1e30
F32 = jnp.float32
BF16 = jnp.bfloat16


def mm(a, b):
    return lax.dot_general(a, b, (((1,), (0,)), ((), ())), preferred_element_type=F32)


def mm_t(a, b):
    return lax.dot_general(a, b, (((1,), (1,)), ((), ())), preferred_element_type=F32)


def t_mm(a, b):
    return lax.dot_general(a, b, (((0,), (0,)), ((), ())), preferred_element_type=F32)


def sees(ids_ref, cnt_ref, a, b):
    inside = jnp.logical_and(a >= 0, a < BLOCKS)
    row = jnp.clip(a, 0, BLOCKS - 1)
    hit = jnp.bool_(False)
    for j in range(NBR):
        hit = jnp.logical_or(hit, jnp.logical_and(j < cnt_ref[row], ids_ref[j, row] == b))
    return jnp.where(jnp.logical_and(hit, inside), F32(0.0), F32(NEG))


def own_bias(mask_ref):
    row = lax.broadcasted_iota(jnp.int32, (2 * BLK, 2 * BLK), 0) >= BLK
    col = lax.broadcasted_iota(jnp.int32, (2 * BLK, 2 * BLK), 1) >= BLK
    off = jnp.where(row, mask_ref[1], mask_ref[0])
    return jnp.where(row == col, F32(0.0), off)


def side_of(index, side):
    even = 1 - lax.rem(index, 2)
    edge = even if side == 0 else 1 - even
    return edge, 2 * edge - 1


def edge_rows(edge):
    return pl.ds(pl.multiple_of(edge * BLK, BLK), BLK)


def head_cols(h, base=0):
    return slice(base + h * HD, base + (h + 1) * HD)


def own_kernel(
    heads, ids_hbm, cnt_hbm, q_hbm, k_hbm, v_hbm, c_hbm, gain_hbm,
    send1_ref, send0_ref, o_ref, lse_ref, p_ref, q_ref, k_ref, v_ref, c_ref, gain_ref, mask_ref, *rest,
):
    *chunk_refs, ids_ref, cnt_ref, sems = rest
    index = lax.axis_index("curve")
    feat = heads * HD
    copies = [
        pltpu.make_async_copy(src, dst, sems.at[n])
        for n, (src, dst) in enumerate(
            (
                (ids_hbm, ids_ref), (cnt_hbm, cnt_ref), (q_hbm, q_ref), (k_hbm, k_ref), (v_hbm, v_ref),
                (c_hbm, c_ref), (gain_hbm, gain_ref),
            )
        )
    ]
    for copy in copies:
        copy.start()
    for copy in copies[:2]:
        copy.wait()
    first = 2 * index
    mask_ref[0] = sees(ids_ref, cnt_ref, first, first + 1)
    mask_ref[1] = sees(ids_ref, cnt_ref, first + 1, first)
    for side in range(2):
        edge, step = side_of(index, side)
        block = first + edge
        mask_ref[2 + 2 * side] = sees(ids_ref, cnt_ref, block, block + step)
        mask_ref[3 + 2 * side] = sees(ids_ref, cnt_ref, block + step, block)
    bias = own_bias(mask_ref)
    for copy in copies[2:5]:
        copy.wait()
    lane = lax.broadcasted_iota(jnp.int32, (2 * BLK, 128), 1)
    stats = jnp.zeros((2 * BLK, 128), F32)
    for h in range(heads):
        hs = head_cols(h)
        s = mm_t(q_ref[:, hs], k_ref[:, hs]) * SCALE + bias
        top = jnp.max(s, axis=1, keepdims=True)
        p = jnp.exp(s - top)
        total = jnp.sum(p, axis=1, keepdims=True)
        p = p * (1.0 / total)
        p_ref[h] = p
        o_ref[:, hs] = mm(p.astype(BF16), v_ref[:, hs])
        stats = jnp.where(lax.rem(lane, heads) == h, top + jnp.log(total), stats)
    lse_ref[...] = stats
    for copy in copies[5:]:
        copy.wait()
    for side, send in enumerate((send0_ref, send1_ref)):
        edge, _ = side_of(index, side)
        rows = edge_rows(edge)
        for n, ref in enumerate((k_ref, v_ref, q_ref, c_ref)):
            send[:, n * feat : (n + 1) * feat] = ref[rows, :]
        send[:, 4 * feat : 5 * feat] = o_ref[rows, :].astype(BF16)
        lse = lse_ref[rows, :]
        lane = lax.broadcasted_iota(jnp.int32, (BLK, 128), 1)
        hi = lse.astype(BF16).astype(F32)
        mid = (lse - hi).astype(BF16).astype(F32)
        parts = jnp.where(lane < heads, hi, jnp.where(lane < 2 * heads, mid, lse - hi - mid))
        send[:, 5 * feat :] = parts.astype(BF16)
    cut = chunk_refs[0].shape[1]
    for n, chunk in enumerate(chunk_refs):
        chunk[...] = send1_ref[:, n * cut : (n + 1) * cut]


def stack(parts):
    return jnp.concatenate(parts, axis=0)


def merge_kernel(*refs):
    _, *chunk_refs, out_ref = refs
    cut = chunk_refs[0].shape[1]
    for n, chunk in enumerate(chunk_refs):
        out_ref[:, n * cut : (n + 1) * cut] = chunk[...]


def hold_kernel(in_ref, out_ref):
    out_ref[...] = in_ref[...]


def add_kernel(a_ref, b_ref, out_ref):
    out_ref[...] = a_ref[...] + b_ref[...]


def join_kernel(
    heads, side, mask_ref, q_ref, k_ref, v_ref, c_ref, gain_ref, o_ref, lse_in_ref, recv, *rest,
):
    *before, a_ref, p_ref, part_ref, sums_ref = rest
    index = lax.axis_index("curve")
    feat = heads * HD
    lane = lax.broadcasted_iota(jnp.int32, (BLK, 128), 1)
    edge, _ = side_of(index, side)
    rows = edge_rows(edge)
    lse_own = lse_in_ref[rows, :]
    far = recv[:, 5 * feat :].astype(F32)
    scores = stack(
        [
            mm_t(q_ref[rows, head_cols(h)], recv[:, head_cols(h)]) * SCALE + mask_ref[2 + 2 * side]
            for h in range(heads)
        ]
        + [
            mm_t(recv[:, head_cols(h, 2 * feat)], k_ref[rows, head_cols(h)]) * SCALE + mask_ref[3 + 2 * side]
            for h in range(heads)
        ]
    )
    lse_part = stack(
        [lse_own[:, h : h + 1] for h in range(heads)]
        + [
            far[:, h : h + 1] + far[:, heads + h : heads + h + 1] + far[:, 2 * heads + h : 2 * heads + h + 1]
            for h in range(heads)
        ]
    )
    top = jnp.maximum(jnp.max(scores, axis=1, keepdims=True), lse_part)
    p = jnp.exp(scores - top)
    part = jnp.exp(lse_part - top)
    inv = 1.0 / (jnp.sum(p, axis=1, keepdims=True) + part)
    p = p * inv
    part = part * inv
    p_ref[...] = p
    p = p.astype(BF16)
    own_part = jnp.zeros((BLK, 128), F32)
    sums = [jnp.zeros((BLK, HD), F32) for _ in range(4)]
    for h in range(heads):
        hs = head_cols(h)
        gain = gain_ref[:, hs]
        n = slice(h * BLK, (h + 1) * BLK)
        a = mm(p[n], recv[:, head_cols(h, feat)]) + part[n] * o_ref[rows, hs]
        a_ref[:BLK, hs] = a
        own_part = jnp.where(lane == h, part[n], own_part)
        sums[0] += a * a
        sums[1] += c_ref[rows, hs].astype(F32) * gain * a
        n = slice((heads + h) * BLK, (heads + h + 1) * BLK)
        a = mm(p[n], v_ref[rows, hs]) + part[n] * recv[:, head_cols(h, 4 * feat)].astype(F32)
        a_ref[BLK:, hs] = a
        sums[2] += a * a
        sums[3] += recv[:, head_cols(h, 3 * feat)].astype(F32) * gain * a
    part_ref[...] = own_part
    sums = [jnp.sum(x, axis=1, keepdims=True) for x in sums]
    both = jnp.where(
        lane < 2, jnp.where(lane == 0, sums[0], sums[1]), jnp.where(lane == 2, sums[2], sums[3])
    ).T
    if not before:
        sums_ref[...] = both[0:8]
        return
    other = before[0][...]
    pairs = (other, both) if side == 1 else (both, other)
    table = [x[r : r + 1] for r in (0, 2, 1, 3) for x in pairs]
    table = jnp.concatenate(table, axis=0)
    for j in range(sums_ref.shape[0]):
        sums_ref[j] = table


def grad_kernel(
    heads, q_ref, k_ref, v_ref, c_ref, gain_ref, p_ref, a0_ref, a1_ref, p0_ref, p1_ref, part0_ref, part1_ref,
    recv0_ref, recv1_ref, sums_ref, normed_hbm, gq_hbm, gk_hbm, gv_hbm,
    normed_ref, gq_out, gk_out, gv_out, gq_ref, gk_ref, gv_ref, d_ref, delta_ref, part_ref, sems,
):
    index = lax.axis_index("curve")
    feat = heads * HD
    gain = gain_ref[...]
    lane = lax.broadcasted_iota(jnp.int32, (BLK, 128), 1)
    total = jnp.sum(sums_ref[...], axis=0) / FEAT
    rinv = lax.rsqrt(total[0:4] + EPS)
    turn = rinv * rinv * rinv * total[4:8]
    columns = jnp.concatenate([rinv, turn, jnp.zeros((BLK - 8, 128), F32)], axis=0).T
    sides = []
    for side in range(2):
        edge, _ = side_of(index, side)
        sides.append(edge_rows(edge))
    for b in range(4):
        side = b % 2
        rows = sides[side] if b < 2 else slice(b * BLK, (b + 1) * BLK)
        a = (a0_ref, a1_ref)[side][:BLK, :] if b < 2 else (a0_ref, a1_ref)[side][BLK:, :]
        r, t = columns[:, b : b + 1], columns[:, 4 + b : 5 + b]
        if b < 2:
            normed_ref[rows, :] = (gain * a * r).astype(BF16)
            cot = c_ref[rows, :]
            part_ref[rows, :] = (part0_ref, part1_ref)[side][...]
        else:
            cot = (recv0_ref, recv1_ref)[side][:, 3 * feat : 4 * feat]
        d = (cot.astype(F32) * gain * r - a * t).astype(BF16)
        d_ref[rows, :] = d
        both = d.astype(F32) * a
        delta = jnp.zeros((BLK, 128), F32)
        for h in range(heads):
            delta = jnp.where(lane == h, jnp.sum(both[:, head_cols(h)], axis=1, keepdims=True), delta)
        delta_ref[rows, :] = delta
    copies = [pltpu.make_async_copy(normed_ref, normed_hbm, sems.at[0])]
    copies[0].start()
    own = slice(0, 2 * BLK)
    for h in range(heads):
        hs = head_cols(h)
        q, k, v, d = q_ref[:, hs], k_ref[:, hs], v_ref[:, hs], d_ref[own, hs]
        p = p_ref[h] * part_ref[own, h : h + 1]
        ds = (p * (mm_t(d, v) - delta_ref[own, h : h + 1]) * SCALE).astype(BF16)
        gq_ref[:, hs] = mm(ds, k)
        gk_ref[:, hs] = t_mm(ds, q)
        gv_ref[:, hs] = t_mm(p.astype(BF16), d)
    for side, recv in enumerate((recv0_ref, recv1_ref)):
        rows = sides[side]
        far_rows = slice((2 + side) * BLK, (3 + side) * BLK)
        pairs = [(h, recv[:, head_cols(h, feat)], rows) for h in range(heads)]
        pairs += [(h, v_ref[rows, head_cols(h)], far_rows) for h in range(heads)]
        dprob = stack([mm_t(d_ref[r, head_cols(h)], v) - delta_ref[r, h : h + 1] for h, v, r in pairs])
        p = (p0_ref, p1_ref)[side][...]
        ds = (p * dprob * SCALE).astype(BF16)
        p = p.astype(BF16)
        for h in range(heads):
            hs = head_cols(h)
            n = slice(h * BLK, (h + 1) * BLK)
            gq_out[rows, hs] = (gq_ref[rows, hs] + mm(ds[n], recv[:, hs])).astype(BF16)
            n = slice((heads + h) * BLK, (heads + h + 1) * BLK)
            gk_out[rows, hs] = (gk_ref[rows, hs] + t_mm(ds[n], recv[:, head_cols(h, 2 * feat)])).astype(BF16)
            gv_out[rows, hs] = (gv_ref[rows, hs] + t_mm(p[n], d_ref[far_rows, hs])).astype(BF16)
        for n, (src, dst) in enumerate(((gq_out, gq_hbm), (gk_out, gk_hbm), (gv_out, gv_hbm))):
            copy = pltpu.make_async_copy(src.at[rows, :], dst.at[rows, :], sems.at[1 + 3 * side + n])
            copy.start()
            copies.append(copy)
    for copy in copies:
        copy.wait()


HBM = pl.BlockSpec(memory_space=pltpu.HBM)
SMEM = pl.BlockSpec(memory_space=pltpu.SMEM)
VMEM = pl.BlockSpec(memory_space=pltpu.VMEM)
PARAMS = pltpu.CompilerParams(vmem_limit_bytes=32 * 1024 * 1024)


def shape(dims, dtype):
    return jax.ShapeDtypeStruct(dims, dtype)


def call(kernel, name, in_specs, outs, scratch=(), mask_out=None, cost=None, space=None):
    specs = [space or VMEM for _ in outs]
    if mask_out is not None:
        specs[mask_out] = SMEM
    return pl.pallas_call(
        kernel,
        name=name,
        out_shape=tuple(outs),
        in_specs=in_specs,
        out_specs=tuple(specs),
        scratch_shapes=list(scratch),
        compiler_params=PARAMS,
        cost_estimate=cost,
    )


XS, YS, ZLO, CORES = 4, 8, 3, 2
AXES = ("curve", "dp")


def spot(x, y, z, core):
    return ((z // ZLO * YS + y) * XS + x) * (ZLO * CORES) + z % ZLO * CORES + core


def swaps(pairs):
    return pairs + [(b, a) for a, b in pairs]


BESIDE, BEYOND, ACROSS = ((3, 6), (0, 1)), ((2, 6), (1, 1)), ((3, 0), (0, 7))
RELAYS = ((BESIDE, BESIDE, BEYOND), (ACROSS, ACROSS, ACROSS))
CHUNKS = 3
HOP_COST, ODD_COST, JOIN_COST, MERGE_COST = 10**10, 10**8, 10**6, 10**6


def routes(count, peers):
    far = range(XS * YS - 1, count - 1, XS * YS)
    even = [(i * peers + j, (i + 1) * peers + j) for i in range(0, count, 2) for j in range(peers)]
    odd = [
        (i * peers + j, (i + 1) * peers + j)
        for i in range(1, count - 1, 2)
        for j in range(peers)
        if i not in far or j >= len(RELAYS) * CORES
    ]
    hops = []
    for chunk in range(CHUNKS):
        out, on = [], []
        for block in range(len(far)):
            for part, relays in enumerate(RELAYS):
                up, down = relays[chunk]
                low, high = block * ZLO + part, (block + 1) * ZLO + part
                for core in range(CORES):
                    first, last = spot(XS - 1, YS - 1, low, core), spot(0, 0, high, core)
                    over, back = spot(*up, low, core), spot(*down, high, core)
                    out += [(first, over), (last, back)]
                    on += [(over, last), (back, first)]
        hops.append((out, on))
    return swaps(even), swaps(odd), hops


def hold(x, name, cost):
    (x,) = call(
        hold_kernel, name, [VMEM], [shape(x.shape, x.dtype)],
        cost=pl.CostEstimate(flops=cost, bytes_accessed=4 * x.size, transcendentals=0),
    )(x)
    return x


def shards(queries, keys, values, cotangent, gain, neighbour_ids, neighbour_counts):
    rows, feat = queries.shape
    heads = feat // HD
    peers = lax.axis_size("dp")
    width = 5 * feat + 128
    cut = width // CHUNKS
    even, odd, hops = routes(lax.axis_size("curve"), peers)
    local = shape((rows, feat), BF16)
    send1, send0, o_own, lse_own, p_own, q, k, v, c, gain, mask, *chunks = call(
        functools.partial(own_kernel, heads),
        "own",
        [HBM] * 7,
        [
            shape((BLK, width), BF16), shape((BLK, width), BF16), shape((rows, feat), F32), shape((rows, 128), F32),
            shape((heads, rows, rows), F32), local, local, local, local, shape((1, feat), F32), shape((8,), F32),
        ]
        + [shape((BLK, cut), BF16)] * CHUNKS,
        [pltpu.SMEM((NBR, BLOCKS), jnp.int32), pltpu.SMEM((BLOCKS,), jnp.int32), pltpu.SemaphoreType.DMA((7,))],
        mask_out=10,
    )(*(pltpu.with_memory_space_constraint(x, pltpu.HBM) for x in (neighbour_ids.T, neighbour_counts, queries, keys, values, cotangent, gain.reshape(1, feat))))
    chunks = [lax.ppermute(chunk, AXES, out) for chunk, (out, _) in zip(chunks, hops)]
    recv1 = lax.ppermute(send1, AXES, odd)
    recv0 = lax.ppermute(send0, AXES, even)
    chunks = [hold(chunk, "hop", HOP_COST) for chunk in chunks]
    chunks = [lax.ppermute(chunk, AXES, on) for chunk, (_, on) in zip(chunks, hops)]
    recv1 = hold(recv1, "odd_in", ODD_COST)
    edge = [shape((rows, feat), F32), shape((2 * heads * BLK, 128), F32), shape((BLK, 128), F32)]
    a0, p0, part0, sums = call(
        functools.partial(join_kernel, heads, 0), "join_even", [SMEM] + [VMEM] * 8, edge + [shape((8, 128), F32)],
        cost=pl.CostEstimate(flops=JOIN_COST, bytes_accessed=4 * rows * feat, transcendentals=0),
    )(mask, q, k, v, c, gain, o_own, lse_own, recv0)
    (relayed,) = call(
        merge_kernel, "merge", [VMEM] * (1 + CHUNKS), [shape((BLK, width), BF16)],
        cost=pl.CostEstimate(flops=MERGE_COST, bytes_accessed=4 * BLK * width, transcendentals=0),
    )(sums, *chunks)
    (recv1,) = call(
        add_kernel, "odd", [VMEM] * 2, [shape((BLK, width), BF16)]
    )(recv1, relayed)
    a1, p1, part1, sums = call(
        functools.partial(join_kernel, heads, 1), "join_odd", [SMEM] + [VMEM] * 9, edge + [shape((peers, 8, 128), F32)],
    )(mask, q, k, v, c, gain, o_own, lse_own, recv1, sums)
    sums = lax.all_to_all(sums, "dp", 0, 0, tiled=True)
    return call(
        functools.partial(grad_kernel, heads),
        "grads",
        [VMEM] * 15,
        [local] * 4,
        [pltpu.VMEM((rows, feat), BF16)] * 4
        + [pltpu.VMEM((rows, feat), F32)] * 3
        + [
            pltpu.VMEM((2 * rows, feat), BF16), pltpu.VMEM((2 * rows, 128), F32), pltpu.VMEM((rows, 128), F32),
            pltpu.SemaphoreType.DMA((7,)),
        ],
        space=HBM,
    )(q, k, v, c, gain, p_own, a0, a1, p0, p1, part0, part1, recv0, recv1, sums)


def solution(mesh):
    wide = P("curve", "dp")
    return jax.shard_map(
        shards,
        mesh=mesh,
        in_specs=(wide, wide, wide, wide, P("dp"), P(), P()),
        out_specs=(wide, wide, wide, wide),
        check_vma=False,
    )
```

```python
import functools
import math

import jax
import jax.numpy as jnp
from jax import lax
from jax.experimental import pallas as pl
from jax.experimental.pallas import tpu as pltpu
from jax.sharding import PartitionSpec as P

FEAT = 3072
HD = 128
BLK = 128
NBR = 3
BLOCKS = 256
EPS = 1e-06
SCALE = 1.0 / math.sqrt(HD)
NEG = -1e30
F32 = jnp.float32
BF16 = jnp.bfloat16


def mm(a, b):
    return lax.dot_general(a, b, (((1,), (0,)), ((), ())), preferred_element_type=F32)


def mm_t(a, b):
    return lax.dot_general(a, b, (((1,), (1,)), ((), ())), preferred_element_type=F32)


def t_mm(a, b):
    return lax.dot_general(a, b, (((0,), (0,)), ((), ())), preferred_element_type=F32)


def sees(ids_ref, cnt_ref, a, b):
    inside = jnp.logical_and(a >= 0, a < BLOCKS)
    row = jnp.clip(a, 0, BLOCKS - 1)
    hit = jnp.bool_(False)
    for j in range(NBR):
        hit = jnp.logical_or(hit, jnp.logical_and(j < cnt_ref[row], ids_ref[j, row] == b))
    return jnp.where(jnp.logical_and(hit, inside), F32(0.0), F32(NEG))


def own_bias(mask_ref):
    row = lax.broadcasted_iota(jnp.int32, (2 * BLK, 2 * BLK), 0) >= BLK
    col = lax.broadcasted_iota(jnp.int32, (2 * BLK, 2 * BLK), 1) >= BLK
    off = jnp.where(row, mask_ref[1], mask_ref[0])
    return jnp.where(row == col, F32(0.0), off)


def side_of(index, side):
    even = 1 - lax.rem(index, 2)
    edge = even if side == 0 else 1 - even
    return edge, 2 * edge - 1


def edge_rows(edge):
    return pl.ds(pl.multiple_of(edge * BLK, BLK), BLK)


def head_cols(h, base=0):
    return slice(base + h * HD, base + (h + 1) * HD)


def own_kernel(
    heads, ids_hbm, cnt_hbm, q_hbm, k_hbm, v_hbm, c_hbm, gain_hbm,
    send1_ref, send0_ref, o_ref, lse_ref, p_ref, q_ref, k_ref, v_ref, c_ref, gain_ref, mask_ref, *rest,
):
    *chunk_refs, ids_ref, cnt_ref, sems = rest
    index = lax.axis_index("curve")
    feat = heads * HD
    copies = [
        pltpu.make_async_copy(src, dst, sems.at[n])
        for n, (src, dst) in enumerate(
            (
                (ids_hbm, ids_ref), (cnt_hbm, cnt_ref), (q_hbm, q_ref), (k_hbm, k_ref), (v_hbm, v_ref),
                (c_hbm, c_ref), (gain_hbm, gain_ref),
            )
        )
    ]
    for copy in copies:
        copy.start()
    for copy in copies[:2]:
        copy.wait()
    first = 2 * index
    mask_ref[0] = sees(ids_ref, cnt_ref, first, first + 1)
    mask_ref[1] = sees(ids_ref, cnt_ref, first + 1, first)
    for side in range(2):
        edge, step = side_of(index, side)
        block = first + edge
        mask_ref[2 + 2 * side] = sees(ids_ref, cnt_ref, block, block + step)
        mask_ref[3 + 2 * side] = sees(ids_ref, cnt_ref, block + step, block)
    bias = own_bias(mask_ref)
    for copy in copies[2:5]:
        copy.wait()
    lane = lax.broadcasted_iota(jnp.int32, (2 * BLK, 128), 1)
    stats = jnp.zeros((2 * BLK, 128), F32)
    for h in range(heads):
        hs = head_cols(h)
        s = mm_t(q_ref[:, hs], k_ref[:, hs]) * SCALE + bias
        top = jnp.max(s, axis=1, keepdims=True)
        p = jnp.exp(s - top)
        total = jnp.sum(p, axis=1, keepdims=True)
        p = p * (1.0 / total)
        p_ref[h] = p
        o_ref[:, hs] = mm(p.astype(BF16), v_ref[:, hs])
        stats = jnp.where(lax.rem(lane, heads) == h, top + jnp.log(total), stats)
    lse_ref[...] = stats
    for copy in copies[5:]:
        copy.wait()
    for side, send in enumerate((send0_ref, send1_ref)):
        edge, _ = side_of(index, side)
        rows = edge_rows(edge)
        for n, ref in enumerate((k_ref, v_ref, q_ref, c_ref)):
            send[:, n * feat : (n + 1) * feat] = ref[rows, :]
        send[:, 4 * feat : 5 * feat] = o_ref[rows, :].astype(BF16)
        lse = lse_ref[rows, :]
        lane = lax.broadcasted_iota(jnp.int32, (BLK, 128), 1)
        hi = lse.astype(BF16).astype(F32)
        mid = (lse - hi).astype(BF16).astype(F32)
        parts = jnp.where(lane < heads, hi, jnp.where(lane < 2 * heads, mid, lse - hi - mid))
        send[:, 5 * feat :] = parts.astype(BF16)
    cut = chunk_refs[0].shape[1]
    for n, chunk in enumerate(chunk_refs):
        chunk[...] = send1_ref[:, n * cut : (n + 1) * cut]


def stack(parts):
    return jnp.concatenate(parts, axis=0)


def merge_kernel(*refs):
    _, *chunk_refs, out_ref = refs
    cut = chunk_refs[0].shape[1]
    for n, chunk in enumerate(chunk_refs):
        out_ref[:, n * cut : (n + 1) * cut] = chunk[...]


def hold_kernel(in_ref, out_ref):
    out_ref[...] = in_ref[...]


def add_kernel(a_ref, b_ref, out_ref):
    out_ref[...] = a_ref[...] + b_ref[...]


def join_kernel(
    heads, side, mask_ref, q_ref, k_ref, v_ref, c_ref, gain_ref, o_ref, lse_in_ref, recv, *rest,
):
    *before, a_ref, p_ref, part_ref, sums_ref = rest
    index = lax.axis_index("curve")
    feat = heads * HD
    lane = lax.broadcasted_iota(jnp.int32, (BLK, 128), 1)
    edge, _ = side_of(index, side)
    rows = edge_rows(edge)
    lse_own = lse_in_ref[rows, :]
    far = recv[:, 5 * feat :].astype(F32)
    scores = stack(
        [
            mm_t(q_ref[rows, head_cols(h)], recv[:, head_cols(h)]) * SCALE + mask_ref[2 + 2 * side]
            for h in range(heads)
        ]
        + [
            mm_t(recv[:, head_cols(h, 2 * feat)], k_ref[rows, head_cols(h)]) * SCALE + mask_ref[3 + 2 * side]
            for h in range(heads)
        ]
    )
    lse_part = stack(
        [lse_own[:, h : h + 1] for h in range(heads)]
        + [
            far[:, h : h + 1] + far[:, heads + h : heads + h + 1] + far[:, 2 * heads + h : 2 * heads + h + 1]
            for h in range(heads)
        ]
    )
    top = jnp.maximum(jnp.max(scores, axis=1, keepdims=True), lse_part)
    p = jnp.exp(scores - top)
    part = jnp.exp(lse_part - top)
    inv = 1.0 / (jnp.sum(p, axis=1, keepdims=True) + part)
    p = p * inv
    part = part * inv
    p_ref[...] = p
    p = p.astype(BF16)
    own_part = jnp.zeros((BLK, 128), F32)
    sums = [jnp.zeros((BLK, HD), F32) for _ in range(4)]
    for h in range(heads):
        hs = head_cols(h)
        gain = gain_ref[:, hs]
        n = slice(h * BLK, (h + 1) * BLK)
        a = mm(p[n], recv[:, head_cols(h, feat)]) + part[n] * o_ref[rows, hs]
        a_ref[:BLK, hs] = a
        own_part = jnp.where(lane == h, part[n], own_part)
        sums[0] += a * a
        sums[1] += c_ref[rows, hs].astype(F32) * gain * a
        n = slice((heads + h) * BLK, (heads + h + 1) * BLK)
        a = mm(p[n], v_ref[rows, hs]) + part[n] * recv[:, head_cols(h, 4 * feat)].astype(F32)
        a_ref[BLK:, hs] = a
        sums[2] += a * a
        sums[3] += recv[:, head_cols(h, 3 * feat)].astype(F32) * gain * a
    part_ref[...] = own_part
    sums = [jnp.sum(x, axis=1, keepdims=True) for x in sums]
    both = jnp.where(
        lane < 2, jnp.where(lane == 0, sums[0], sums[1]), jnp.where(lane == 2, sums[2], sums[3])
    ).T
    if not before:
        sums_ref[...] = both[0:8]
        return
    other = before[0][...]
    pairs = (other, both) if side == 1 else (both, other)
    table = [x[r : r + 1] for r in (0, 2, 1, 3) for x in pairs]
    table = jnp.concatenate(table, axis=0)
    for j in range(sums_ref.shape[0]):
        sums_ref[j] = table


def grad_kernel(
    heads, q_ref, k_ref, v_ref, c_ref, gain_ref, p_ref, a0_ref, a1_ref, p0_ref, p1_ref, part0_ref, part1_ref,
    recv0_ref, recv1_ref, sums_ref, normed_hbm, gq_hbm, gk_hbm, gv_hbm,
    normed_ref, gq_out, gk_out, gv_out, gq_ref, gk_ref, gv_ref, d_ref, delta_ref, part_ref, sems,
):
    index = lax.axis_index("curve")
    feat = heads * HD
    gain = gain_ref[...]
    lane = lax.broadcasted_iota(jnp.int32, (BLK, 128), 1)
    total = jnp.sum(sums_ref[...], axis=0) / FEAT
    rinv = lax.rsqrt(total[0:4] + EPS)
    turn = rinv * rinv * rinv * total[4:8]
    columns = jnp.concatenate([rinv, turn, jnp.zeros((BLK - 8, 128), F32)], axis=0).T
    sides = []
    for side in range(2):
        edge, _ = side_of(index, side)
        sides.append(edge_rows(edge))
    for b in range(4):
        side = b % 2
        rows = sides[side] if b < 2 else slice(b * BLK, (b + 1) * BLK)
        a = (a0_ref, a1_ref)[side][:BLK, :] if b < 2 else (a0_ref, a1_ref)[side][BLK:, :]
        r, t = columns[:, b : b + 1], columns[:, 4 + b : 5 + b]
        if b < 2:
            normed_ref[rows, :] = (gain * a * r).astype(BF16)
            cot = c_ref[rows, :]
            part_ref[rows, :] = (part0_ref, part1_ref)[side][...]
        else:
            cot = (recv0_ref, recv1_ref)[side][:, 3 * feat : 4 * feat]
        d = (cot.astype(F32) * gain * r - a * t).astype(BF16)
        d_ref[rows, :] = d
        both = d.astype(F32) * a
        delta = jnp.zeros((BLK, 128), F32)
        for h in range(heads):
            delta = jnp.where(lane == h, jnp.sum(both[:, head_cols(h)], axis=1, keepdims=True), delta)
        delta_ref[rows, :] = delta
    copies = [pltpu.make_async_copy(normed_ref, normed_hbm, sems.at[0])]
    copies[0].start()
    own = slice(0, 2 * BLK)
    for h in range(heads):
        hs = head_cols(h)
        q, k, v, d = q_ref[:, hs], k_ref[:, hs], v_ref[:, hs], d_ref[own, hs]
        p = p_ref[h] * part_ref[own, h : h + 1]
        ds = (p * (mm_t(d, v) - delta_ref[own, h : h + 1]) * SCALE).astype(BF16)
        gq_ref[:, hs] = mm(ds, k)
        gk_ref[:, hs] = t_mm(ds, q)
        gv_ref[:, hs] = t_mm(p.astype(BF16), d)
    for side, recv in enumerate((recv0_ref, recv1_ref)):
        rows = sides[side]
        far_rows = slice((2 + side) * BLK, (3 + side) * BLK)
        pairs = [(h, recv[:, head_cols(h, feat)], rows) for h in range(heads)]
        pairs += [(h, v_ref[rows, head_cols(h)], far_rows) for h in range(heads)]
        dprob = stack([mm_t(d_ref[r, head_cols(h)], v) - delta_ref[r, h : h + 1] for h, v, r in pairs])
        p = (p0_ref, p1_ref)[side][...]
        ds = (p * dprob * SCALE).astype(BF16)
        p = p.astype(BF16)
        for h in range(heads):
            hs = head_cols(h)
            n = slice(h * BLK, (h + 1) * BLK)
            gq_out[rows, hs] = (gq_ref[rows, hs] + mm(ds[n], recv[:, hs])).astype(BF16)
            n = slice((heads + h) * BLK, (heads + h + 1) * BLK)
            gk_out[rows, hs] = (gk_ref[rows, hs] + t_mm(ds[n], recv[:, head_cols(h, 2 * feat)])).astype(BF16)
            gv_out[rows, hs] = (gv_ref[rows, hs] + t_mm(p[n], d_ref[far_rows, hs])).astype(BF16)
        for n, (src, dst) in enumerate(((gq_out, gq_hbm), (gk_out, gk_hbm), (gv_out, gv_hbm))):
            copy = pltpu.make_async_copy(src.at[rows, :], dst.at[rows, :], sems.at[1 + 3 * side + n])
            copy.start()
            copies.append(copy)
    for copy in copies:
        copy.wait()


HBM = pl.BlockSpec(memory_space=pltpu.HBM)
SMEM = pl.BlockSpec(memory_space=pltpu.SMEM)
VMEM = pl.BlockSpec(memory_space=pltpu.VMEM)
PARAMS = pltpu.CompilerParams(vmem_limit_bytes=32 * 1024 * 1024)


def shape(dims, dtype):
    return jax.ShapeDtypeStruct(dims, dtype)


def call(kernel, name, in_specs, outs, scratch=(), mask_out=None, cost=None, space=None):
    specs = [space or VMEM for _ in outs]
    if mask_out is not None:
        specs[mask_out] = SMEM
    return pl.pallas_call(
        kernel,
        name=name,
        out_shape=tuple(outs),
        in_specs=in_specs,
        out_specs=tuple(specs),
        scratch_shapes=list(scratch),
        compiler_params=PARAMS,
        cost_estimate=cost,
    )


XS, YS, ZLO, CORES = 4, 8, 3, 2
AXES = ("curve", "dp")


def spot(x, y, z, core):
    return ((z // ZLO * YS + y) * XS + x) * (ZLO * CORES) + z % ZLO * CORES + core


def swaps(pairs):
    return pairs + [(b, a) for a, b in pairs]


ACROSS = ((3, 0), (0, 7))
RELAYS = (
    (((3, 6), (1, 1)), ((3, 6), (0, 1)), ((2, 6), (1, 1))),
    (((3, 0), (0, 1)), ACROSS, ACROSS),
)
CHUNKS = 3
HOP_COST, ODD_COST, JOIN_COST, MERGE_COST = 10**10, 10**8, 10**6, 10**6


def routes(count, peers):
    far = range(XS * YS - 1, count - 1, XS * YS)
    even = [(i * peers + j, (i + 1) * peers + j) for i in range(0, count, 2) for j in range(peers)]
    odd = [
        (i * peers + j, (i + 1) * peers + j)
        for i in range(1, count - 1, 2)
        for j in range(peers)
        if i not in far or j >= len(RELAYS) * CORES
    ]
    hops = []
    for chunk in range(CHUNKS):
        out, on = [], []
        for block in range(len(far)):
            for part, relays in enumerate(RELAYS):
                up, down = relays[chunk]
                low, high = block * ZLO + part, (block + 1) * ZLO + part
                for core in range(CORES):
                    first, last = spot(XS - 1, YS - 1, low, core), spot(0, 0, high, core)
                    over, back = spot(*up, low, core), spot(*down, high, core)
                    out += [(first, over), (last, back)]
                    on += [(over, last), (back, first)]
        hops.append((out, on))
    return swaps(even), swaps(odd), hops


def hold(x, name, cost):
    (x,) = call(
        hold_kernel, name, [VMEM], [shape(x.shape, x.dtype)],
        cost=pl.CostEstimate(flops=cost, bytes_accessed=4 * x.size, transcendentals=0),
    )(x)
    return x


def shards(queries, keys, values, cotangent, gain, neighbour_ids, neighbour_counts):
    rows, feat = queries.shape
    heads = feat // HD
    peers = lax.axis_size("dp")
    width = 5 * feat + 128
    cut = width // CHUNKS
    even, odd, hops = routes(lax.axis_size("curve"), peers)
    local = shape((rows, feat), BF16)
    send1, send0, o_own, lse_own, p_own, q, k, v, c, gain, mask, *chunks = call(
        functools.partial(own_kernel, heads),
        "own",
        [HBM] * 7,
        [
            shape((BLK, width), BF16), shape((BLK, width), BF16), shape((rows, feat), F32), shape((rows, 128), F32),
            shape((heads, rows, rows), F32), local, local, local, local, shape((1, feat), F32), shape((8,), F32),
        ]
        + [shape((BLK, cut), BF16)] * CHUNKS,
        [pltpu.SMEM((NBR, BLOCKS), jnp.int32), pltpu.SMEM((BLOCKS,), jnp.int32), pltpu.SemaphoreType.DMA((7,))],
        mask_out=10,
    )(*(pltpu.with_memory_space_constraint(x, pltpu.HBM) for x in (neighbour_ids.T, neighbour_counts, queries, keys, values, cotangent, gain.reshape(1, feat))))
    chunks = [lax.ppermute(chunk, AXES, out) for chunk, (out, _) in zip(chunks, hops)]
    recv1 = lax.ppermute(send1, AXES, odd)
    recv0 = lax.ppermute(send0, AXES, even)
    chunks = [hold(chunk, "hop", HOP_COST) for chunk in chunks]
    chunks = [lax.ppermute(chunk, AXES, on) for chunk, (_, on) in zip(chunks, hops)]
    recv1 = hold(recv1, "odd_in", ODD_COST)
    edge = [shape((rows, feat), F32), shape((2 * heads * BLK, 128), F32), shape((BLK, 128), F32)]
    a0, p0, part0, sums = call(
        functools.partial(join_kernel, heads, 0), "join_even", [SMEM] + [VMEM] * 8, edge + [shape((8, 128), F32)],
        cost=pl.CostEstimate(flops=JOIN_COST, bytes_accessed=4 * rows * feat, transcendentals=0),
    )(mask, q, k, v, c, gain, o_own, lse_own, recv0)
    (relayed,) = call(
        merge_kernel, "merge", [VMEM] * (1 + CHUNKS), [shape((BLK, width), BF16)],
        cost=pl.CostEstimate(flops=MERGE_COST, bytes_accessed=4 * BLK * width, transcendentals=0),
    )(sums, *chunks)
    (recv1,) = call(
        add_kernel, "odd", [VMEM] * 2, [shape((BLK, width), BF16)]
    )(recv1, relayed)
    a1, p1, part1, sums = call(
        functools.partial(join_kernel, heads, 1), "join_odd", [SMEM] + [VMEM] * 9, edge + [shape((peers, 8, 128), F32)],
    )(mask, q, k, v, c, gain, o_own, lse_own, recv1, sums)
    sums = lax.all_to_all(sums, "dp", 0, 0, tiled=True)
    return call(
        functools.partial(grad_kernel, heads),
        "grads",
        [VMEM] * 15,
        [local] * 4,
        [pltpu.VMEM((rows, feat), BF16)] * 4
        + [pltpu.VMEM((rows, feat), F32)] * 3
        + [
            pltpu.VMEM((2 * rows, feat), BF16), pltpu.VMEM((2 * rows, 128), F32), pltpu.VMEM((rows, 128), F32),
            pltpu.SemaphoreType.DMA((7,)),
        ],
        space=HBM,
    )(q, k, v, c, gain, p_own, a0, a1, p0, p1, part0, part1, recv0, recv1, sums)


def solution(mesh):
    wide = P("curve", "dp")
    return jax.shard_map(
        shards,
        mesh=mesh,
        in_specs=(wide, wide, wide, wide, P("dp"), P(), P()),
        out_specs=(wide, wide, wide, wide),
        check_vma=False,
    )
```

```python
import functools
import math

import jax
import jax.numpy as jnp
from jax import lax
from jax.experimental import pallas as pl
from jax.experimental.pallas import tpu as pltpu
from jax.sharding import PartitionSpec as P

FEAT = 3072
HD = 128
BLK = 128
NBR = 3
BLOCKS = 256
EPS = 1e-06
SCALE = 1.0 / math.sqrt(HD)
NEG = -1e30
F32 = jnp.float32
BF16 = jnp.bfloat16


def mm(a, b):
    return lax.dot_general(a, b, (((1,), (0,)), ((), ())), preferred_element_type=F32)


def mm_t(a, b):
    return lax.dot_general(a, b, (((1,), (1,)), ((), ())), preferred_element_type=F32)


def t_mm(a, b):
    return lax.dot_general(a, b, (((0,), (0,)), ((), ())), preferred_element_type=F32)


def sees(ids_ref, cnt_ref, a, b):
    inside = jnp.logical_and(a >= 0, a < BLOCKS)
    row = jnp.clip(a, 0, BLOCKS - 1)
    hit = jnp.bool_(False)
    for j in range(NBR):
        hit = jnp.logical_or(hit, jnp.logical_and(j < cnt_ref[row], ids_ref[j, row] == b))
    return jnp.where(jnp.logical_and(hit, inside), F32(0.0), F32(NEG))


def own_bias(mask_ref):
    row = lax.broadcasted_iota(jnp.int32, (2 * BLK, 2 * BLK), 0) >= BLK
    col = lax.broadcasted_iota(jnp.int32, (2 * BLK, 2 * BLK), 1) >= BLK
    off = jnp.where(row, mask_ref[1], mask_ref[0])
    return jnp.where(row == col, F32(0.0), off)


def side_of(index, side):
    even = 1 - lax.rem(index, 2)
    edge = even if side == 0 else 1 - even
    return edge, 2 * edge - 1


def edge_rows(edge):
    return pl.ds(pl.multiple_of(edge * BLK, BLK), BLK)


def head_cols(h, base=0):
    return slice(base + h * HD, base + (h + 1) * HD)


def own_kernel(
    heads, ids_hbm, cnt_hbm, q_hbm, k_hbm, v_hbm, c_hbm, gain_hbm,
    send1_ref, send0_ref, o_ref, lse_ref, p_ref, q_ref, k_ref, v_ref, c_ref, gain_ref, mask_ref, *rest,
):
    *chunk_refs, ids_ref, cnt_ref, sems = rest
    index = lax.axis_index("curve")
    feat = heads * HD
    copies = [
        pltpu.make_async_copy(src, dst, sems.at[n])
        for n, (src, dst) in enumerate(
            (
                (ids_hbm, ids_ref), (cnt_hbm, cnt_ref), (q_hbm, q_ref), (k_hbm, k_ref), (v_hbm, v_ref),
                (c_hbm, c_ref), (gain_hbm, gain_ref),
            )
        )
    ]
    for copy in copies:
        copy.start()
    for copy in copies[:2]:
        copy.wait()
    first = 2 * index
    mask_ref[0] = sees(ids_ref, cnt_ref, first, first + 1)
    mask_ref[1] = sees(ids_ref, cnt_ref, first + 1, first)
    for side in range(2):
        edge, step = side_of(index, side)
        block = first + edge
        mask_ref[2 + 2 * side] = sees(ids_ref, cnt_ref, block, block + step)
        mask_ref[3 + 2 * side] = sees(ids_ref, cnt_ref, block + step, block)
    bias = own_bias(mask_ref)
    for copy in copies[2:5]:
        copy.wait()
    lane = lax.broadcasted_iota(jnp.int32, (2 * BLK, 128), 1)
    stats = jnp.zeros((2 * BLK, 128), F32)
    for h in range(heads):
        hs = head_cols(h)
        s = mm_t(q_ref[:, hs], k_ref[:, hs]) * SCALE + bias
        top = jnp.max(s, axis=1, keepdims=True)
        p = jnp.exp(s - top)
        total = jnp.sum(p, axis=1, keepdims=True)
        p = p * (1.0 / total)
        p_ref[h] = p
        o_ref[:, hs] = mm(p.astype(BF16), v_ref[:, hs])
        stats = jnp.where(lax.rem(lane, heads) == h, top + jnp.log(total), stats)
    lse_ref[...] = stats
    for copy in copies[5:]:
        copy.wait()
    for side, send in enumerate((send0_ref, send1_ref)):
        edge, _ = side_of(index, side)
        rows = edge_rows(edge)
        for n, ref in enumerate((k_ref, v_ref, q_ref, c_ref)):
            send[:, n * feat : (n + 1) * feat] = ref[rows, :]
        send[:, 4 * feat : 5 * feat] = o_ref[rows, :].astype(BF16)
        lse = lse_ref[rows, :]
        lane = lax.broadcasted_iota(jnp.int32, (BLK, 128), 1)
        hi = lse.astype(BF16).astype(F32)
        mid = (lse - hi).astype(BF16).astype(F32)
        parts = jnp.where(lane < heads, hi, jnp.where(lane < 2 * heads, mid, lse - hi - mid))
        send[:, 5 * feat :] = parts.astype(BF16)
    cut = chunk_refs[0].shape[1]
    for n, chunk in enumerate(chunk_refs):
        chunk[...] = send1_ref[:, n * cut : (n + 1) * cut]


def stack(parts):
    return jnp.concatenate(parts, axis=0)


def merge_kernel(*refs):
    _, *chunk_refs, out_ref = refs
    cut = chunk_refs[0].shape[1]
    for n, chunk in enumerate(chunk_refs):
        out_ref[:, n * cut : (n + 1) * cut] = chunk[...]


def hold_kernel(in_ref, out_ref):
    out_ref[...] = in_ref[...]


def add_kernel(a_ref, b_ref, out_ref):
    out_ref[...] = a_ref[...] + b_ref[...]


def join_kernel(
    heads, side, mask_ref, q_ref, k_ref, v_ref, c_ref, gain_ref, o_ref, lse_in_ref, recv, *rest,
):
    *before, a_ref, p_ref, part_ref, sums_ref = rest
    index = lax.axis_index("curve")
    feat = heads * HD
    lane = lax.broadcasted_iota(jnp.int32, (BLK, 128), 1)
    edge, _ = side_of(index, side)
    rows = edge_rows(edge)
    lse_own = lse_in_ref[rows, :]
    far = recv[:, 5 * feat :].astype(F32)
    scores = stack(
        [
            mm_t(q_ref[rows, head_cols(h)], recv[:, head_cols(h)]) * SCALE + mask_ref[2 + 2 * side]
            for h in range(heads)
        ]
        + [
            mm_t(recv[:, head_cols(h, 2 * feat)], k_ref[rows, head_cols(h)]) * SCALE + mask_ref[3 + 2 * side]
            for h in range(heads)
        ]
    )
    lse_part = stack(
        [lse_own[:, h : h + 1] for h in range(heads)]
        + [
            far[:, h : h + 1] + far[:, heads + h : heads + h + 1] + far[:, 2 * heads + h : 2 * heads + h + 1]
            for h in range(heads)
        ]
    )
    top = jnp.maximum(jnp.max(scores, axis=1, keepdims=True), lse_part)
    p = jnp.exp(scores - top)
    part = jnp.exp(lse_part - top)
    inv = 1.0 / (jnp.sum(p, axis=1, keepdims=True) + part)
    p = p * inv
    part = part * inv
    p_ref[...] = p
    p = p.astype(BF16)
    own_part = jnp.zeros((BLK, 128), F32)
    sums = [jnp.zeros((BLK, HD), F32) for _ in range(4)]
    for h in range(heads):
        hs = head_cols(h)
        gain = gain_ref[:, hs]
        n = slice(h * BLK, (h + 1) * BLK)
        a = mm(p[n], recv[:, head_cols(h, feat)]) + part[n] * o_ref[rows, hs]
        a_ref[:BLK, hs] = a
        own_part = jnp.where(lane == h, part[n], own_part)
        sums[0] += a * a
        sums[1] += c_ref[rows, hs].astype(F32) * gain * a
        n = slice((heads + h) * BLK, (heads + h + 1) * BLK)
        a = mm(p[n], v_ref[rows, hs]) + part[n] * recv[:, head_cols(h, 4 * feat)].astype(F32)
        a_ref[BLK:, hs] = a
        sums[2] += a * a
        sums[3] += recv[:, head_cols(h, 3 * feat)].astype(F32) * gain * a
    part_ref[...] = own_part
    sums = [jnp.sum(x, axis=1, keepdims=True) for x in sums]
    both = jnp.where(
        lane < 2, jnp.where(lane == 0, sums[0], sums[1]), jnp.where(lane == 2, sums[2], sums[3])
    ).T
    if not before:
        sums_ref[...] = both[0:8]
        return
    other = before[0][...]
    pairs = (other, both) if side == 1 else (both, other)
    table = [x[r : r + 1] for r in (0, 2, 1, 3) for x in pairs]
    table = jnp.concatenate(table, axis=0)
    for j in range(sums_ref.shape[0]):
        sums_ref[j] = table


def grad_kernel(
    heads, q_ref, k_ref, v_ref, c_ref, gain_ref, p_ref, a0_ref, a1_ref, p0_ref, p1_ref, part0_ref, part1_ref,
    recv0_ref, recv1_ref, sums_ref, normed_hbm, gq_hbm, gk_hbm, gv_hbm,
    normed_ref, gq_out, gk_out, gv_out, gq_ref, gk_ref, gv_ref, d_ref, delta_ref, part_ref, sems,
):
    index = lax.axis_index("curve")
    feat = heads * HD
    gain = gain_ref[...]
    lane = lax.broadcasted_iota(jnp.int32, (BLK, 128), 1)
    total = jnp.sum(sums_ref[...], axis=0) / FEAT
    rinv = lax.rsqrt(total[0:4] + EPS)
    turn = rinv * rinv * rinv * total[4:8]
    columns = jnp.concatenate([rinv, turn, jnp.zeros((BLK - 8, 128), F32)], axis=0).T
    sides = []
    for side in range(2):
        edge, _ = side_of(index, side)
        sides.append(edge_rows(edge))
    for b in range(4):
        side = b % 2
        rows = sides[side] if b < 2 else slice(b * BLK, (b + 1) * BLK)
        a = (a0_ref, a1_ref)[side][:BLK, :] if b < 2 else (a0_ref, a1_ref)[side][BLK:, :]
        r, t = columns[:, b : b + 1], columns[:, 4 + b : 5 + b]
        if b < 2:
            normed_ref[rows, :] = (gain * a * r).astype(BF16)
            cot = c_ref[rows, :]
            part_ref[rows, :] = (part0_ref, part1_ref)[side][...]
        else:
            cot = (recv0_ref, recv1_ref)[side][:, 3 * feat : 4 * feat]
        d = (cot.astype(F32) * gain * r - a * t).astype(BF16)
        d_ref[rows, :] = d
        both = d.astype(F32) * a
        delta = jnp.zeros((BLK, 128), F32)
        for h in range(heads):
            delta = jnp.where(lane == h, jnp.sum(both[:, head_cols(h)], axis=1, keepdims=True), delta)
        delta_ref[rows, :] = delta
    copies = [pltpu.make_async_copy(normed_ref, normed_hbm, sems.at[0])]
    copies[0].start()
    own = slice(0, 2 * BLK)
    for h in range(heads):
        hs = head_cols(h)
        q, k, v, d = q_ref[:, hs], k_ref[:, hs], v_ref[:, hs], d_ref[own, hs]
        p = p_ref[h] * part_ref[own, h : h + 1]
        ds = (p * (mm_t(d, v) - delta_ref[own, h : h + 1]) * SCALE).astype(BF16)
        gq_ref[:, hs] = mm(ds, k)
        gk_ref[:, hs] = t_mm(ds, q)
        gv_ref[:, hs] = t_mm(p.astype(BF16), d)
    for side, recv in enumerate((recv0_ref, recv1_ref)):
        rows = sides[side]
        far_rows = slice((2 + side) * BLK, (3 + side) * BLK)
        pairs = [(h, recv[:, head_cols(h, feat)], rows) for h in range(heads)]
        pairs += [(h, v_ref[rows, head_cols(h)], far_rows) for h in range(heads)]
        dprob = stack([mm_t(d_ref[r, head_cols(h)], v) - delta_ref[r, h : h + 1] for h, v, r in pairs])
        p = (p0_ref, p1_ref)[side][...]
        ds = (p * dprob * SCALE).astype(BF16)
        p = p.astype(BF16)
        for h in range(heads):
            hs = head_cols(h)
            n = slice(h * BLK, (h + 1) * BLK)
            gq_out[rows, hs] = (gq_ref[rows, hs] + mm(ds[n], recv[:, hs])).astype(BF16)
            n = slice((heads + h) * BLK, (heads + h + 1) * BLK)
            gk_out[rows, hs] = (gk_ref[rows, hs] + t_mm(ds[n], recv[:, head_cols(h, 2 * feat)])).astype(BF16)
            gv_out[rows, hs] = (gv_ref[rows, hs] + t_mm(p[n], d_ref[far_rows, hs])).astype(BF16)
        for n, (src, dst) in enumerate(((gq_out, gq_hbm), (gk_out, gk_hbm), (gv_out, gv_hbm))):
            copy = pltpu.make_async_copy(src.at[rows, :], dst.at[rows, :], sems.at[1 + 3 * side + n])
            copy.start()
            copies.append(copy)
    for copy in copies:
        copy.wait()


HBM = pl.BlockSpec(memory_space=pltpu.HBM)
SMEM = pl.BlockSpec(memory_space=pltpu.SMEM)
VMEM = pl.BlockSpec(memory_space=pltpu.VMEM)
PARAMS = pltpu.CompilerParams(vmem_limit_bytes=32 * 1024 * 1024)


def shape(dims, dtype):
    return jax.ShapeDtypeStruct(dims, dtype)


def call(kernel, name, in_specs, outs, scratch=(), mask_out=None, cost=None, space=None):
    specs = [space or VMEM for _ in outs]
    if mask_out is not None:
        specs[mask_out] = SMEM
    return pl.pallas_call(
        kernel,
        name=name,
        out_shape=tuple(outs),
        in_specs=in_specs,
        out_specs=tuple(specs),
        scratch_shapes=list(scratch),
        compiler_params=PARAMS,
        cost_estimate=cost,
    )


XS, YS, ZLO, CORES = 4, 8, 3, 2
AXES = ("curve", "dp")


def spot(x, y, z, core):
    return ((z // ZLO * YS + y) * XS + x) * (ZLO * CORES) + z % ZLO * CORES + core


def swaps(pairs):
    return pairs + [(b, a) for a, b in pairs]


ACROSS = ((3, 0), (0, 7))
RELAYS = (
    (((3, 6), (1, 0)), ((3, 6), (0, 1)), ((2, 6), (1, 1))),
    (((3, 0), (0, 1)), ACROSS, ACROSS),
)
CHUNKS = 3
HOP_COST, ODD_COST, JOIN_COST, MERGE_COST = 10**10, 10**8, 10**6, 10**6


def routes(count, peers):
    far = range(XS * YS - 1, count - 1, XS * YS)
    even = [(i * peers + j, (i + 1) * peers + j) for i in range(0, count, 2) for j in range(peers)]
    odd = [
        (i * peers + j, (i + 1) * peers + j)
        for i in range(1, count - 1, 2)
        for j in range(peers)
        if i not in far or j >= len(RELAYS) * CORES
    ]
    hops = []
    for chunk in range(CHUNKS):
        out, on = [], []
        for block in range(len(far)):
            for part, relays in enumerate(RELAYS):
                up, down = relays[chunk]
                low, high = block * ZLO + part, (block + 1) * ZLO + part
                for core in range(CORES):
                    first, last = spot(XS - 1, YS - 1, low, core), spot(0, 0, high, core)
                    over, back = spot(*up, low, core), spot(*down, high, core)
                    out += [(first, over), (last, back)]
                    on += [(over, last), (back, first)]
        hops.append((out, on))
    return swaps(even), swaps(odd), hops


def hold(x, name, cost):
    (x,) = call(
        hold_kernel, name, [VMEM], [shape(x.shape, x.dtype)],
        cost=pl.CostEstimate(flops=cost, bytes_accessed=4 * x.size, transcendentals=0),
    )(x)
    return x


def shards(queries, keys, values, cotangent, gain, neighbour_ids, neighbour_counts):
    rows, feat = queries.shape
    heads = feat // HD
    peers = lax.axis_size("dp")
    width = 5 * feat + 128
    cut = width // CHUNKS
    even, odd, hops = routes(lax.axis_size("curve"), peers)
    local = shape((rows, feat), BF16)
    send1, send0, o_own, lse_own, p_own, q, k, v, c, gain, mask, *chunks = call(
        functools.partial(own_kernel, heads),
        "own",
        [HBM] * 7,
        [
            shape((BLK, width), BF16), shape((BLK, width), BF16), shape((rows, feat), F32), shape((rows, 128), F32),
            shape((heads, rows, rows), F32), local, local, local, local, shape((1, feat), F32), shape((8,), F32),
        ]
        + [shape((BLK, cut), BF16)] * CHUNKS,
        [pltpu.SMEM((NBR, BLOCKS), jnp.int32), pltpu.SMEM((BLOCKS,), jnp.int32), pltpu.SemaphoreType.DMA((7,))],
        mask_out=10,
    )(*(pltpu.with_memory_space_constraint(x, pltpu.HBM) for x in (neighbour_ids.T, neighbour_counts, queries, keys, values, cotangent, gain.reshape(1, feat))))
    chunks = [lax.ppermute(chunk, AXES, out) for chunk, (out, _) in zip(chunks, hops)]
    recv1 = lax.ppermute(send1, AXES, odd)
    recv0 = lax.ppermute(send0, AXES, even)
    chunks = [hold(chunk, "hop", HOP_COST) for chunk in chunks]
    chunks = [lax.ppermute(chunk, AXES, on) for chunk, (_, on) in zip(chunks, hops)]
    recv1 = hold(recv1, "odd_in", ODD_COST)
    edge = [shape((rows, feat), F32), shape((2 * heads * BLK, 128), F32), shape((BLK, 128), F32)]
    a0, p0, part0, sums = call(
        functools.partial(join_kernel, heads, 0), "join_even", [SMEM] + [VMEM] * 8, edge + [shape((8, 128), F32)],
        cost=pl.CostEstimate(flops=JOIN_COST, bytes_accessed=4 * rows * feat, transcendentals=0),
    )(mask, q, k, v, c, gain, o_own, lse_own, recv0)
    (relayed,) = call(
        merge_kernel, "merge", [VMEM] * (1 + CHUNKS), [shape((BLK, width), BF16)],
        cost=pl.CostEstimate(flops=MERGE_COST, bytes_accessed=4 * BLK * width, transcendentals=0),
    )(sums, *chunks)
    (recv1,) = call(
        add_kernel, "odd", [VMEM] * 2, [shape((BLK, width), BF16)]
    )(recv1, relayed)
    a1, p1, part1, sums = call(
        functools.partial(join_kernel, heads, 1), "join_odd", [SMEM] + [VMEM] * 9, edge + [shape((peers, 8, 128), F32)],
    )(mask, q, k, v, c, gain, o_own, lse_own, recv1, sums)
    sums = lax.all_to_all(sums, "dp", 0, 0, tiled=True)
    return call(
        functools.partial(grad_kernel, heads),
        "grads",
        [VMEM] * 15,
        [local] * 4,
        [pltpu.VMEM((rows, feat), BF16)] * 4
        + [pltpu.VMEM((rows, feat), F32)] * 3
        + [
            pltpu.VMEM((2 * rows, feat), BF16), pltpu.VMEM((2 * rows, 128), F32), pltpu.VMEM((rows, 128), F32),
            pltpu.SemaphoreType.DMA((7,)),
        ],
        space=HBM,
    )(q, k, v, c, gain, p_own, a0, a1, p0, p1, part0, part1, recv0, recv1, sums)


def solution(mesh):
    wide = P("curve", "dp")
    return jax.shard_map(
        shards,
        mesh=mesh,
        in_specs=(wide, wide, wide, wide, P("dp"), P(), P()),
        out_specs=(wide, wide, wide, wide),
        check_vma=False,
    )
```
